32 devices in a mesh: fsdp: 4 (over z), bal: 8 (over y, x, core).
Axes of the slice: x: 2, y: 2, z: 4, core: 2. Of those that a mesh axis runs over, the one named last changes fastest.
Arguments:
- tokens: bfloat16 [4096, 2048], P(('fsdp', 'bal')), may hold values from -6 to 6
- kv_weight: bfloat16 [2048, 1024], P('fsdp')
- queries: bfloat16 [4096, 2048], P(('fsdp', 'bal')), may hold values from -300 to 300
- out_grad: bfloat16 [4096, 2048], P(('fsdp', 'bal')), may hold values from -6 to 6
- doc_lengths: int32 [4, 4], P('fsdp'), may hold values from 1 to 512, 1024 in all within a row
Outputs:
- attn_out: bfloat16 [4096, 2048], P(('fsdp', 'bal'))
- grad_queries: bfloat16 [4096, 2048], P(('fsdp', 'bal'))
- grad_tokens: bfloat16 [4096, 2048], P(('fsdp', 'bal'))
- grad_kv_weight: float32 [2048, 1024], P('fsdp')
The draws below stay inside these ranges and needn't reach their ends.
Inputs may be any that keep to these rules, and one draw needn't show every extreme that they name: Each row of doc_lengths sums to 1024, and its largest entry is exactly 512.
All inputs are finite; a program needn't handle non-finite values.
Results may differ from the reference program's by a relative error of at most 0.015.
Values may be sent and summed in bfloat16 or wider, within the bound.
No kernel may reach another device: no remote copies, remote signals or barrier semaphores. Data moves between devices by JAX's collectives and lax.ppermute only.
A program may use at most 64 MiB of HBM per device.

```python
import math
import jax
import jax.numpy as jnp
import numpy as np
from jax import lax

D = 2048
HEADS = 16
KV_HEADS = 4
HEAD_DIM = 128
TOK_DEV = 128
REACH = 4
DOC_MOST = 512
SEQ = 1024
GROUPS = 4
DOCS = 4
TOKENS = 4096
KV_WIDTH = 1024
Q_WIDTH = 2048
N_FSDP = 4
N_BAL = 8


def dense_inputs(key):
    tokens = jnp.clip(jax.random.normal(jax.random.fold_in(key, 11), (TOKENS, D), jnp.float32), -6.0, 6.0)
    weight = jax.random.normal(jax.random.fold_in(key, 12), (D, KV_WIDTH), jnp.float32) * D ** (-0.5)
    return (tokens, weight)


def draw_tokens(key, part):
    return dense_inputs(key)[0].astype(jnp.bfloat16)


def draw_kv_weight(key, part):
    return dense_inputs(key)[1].astype(jnp.bfloat16)


def draw_queries(key, part):
    draw_base = jnp.clip(jax.random.normal(jax.random.fold_in(key, 13), (TOKENS, HEADS * HEAD_DIM), jnp.float32), -6.0, 6.0)
    return draw_base.astype(jnp.bfloat16)


def level_of(stream_key, extent, split, least, top_value):
    def one(position, parts):
        heights = jax.random.uniform(jax.random.fold_in(jax.random.fold_in(stream_key, 6), position), (parts,), jnp.float32, least / len(split), top_value / len(split))
        return jnp.repeat(jnp.exp(heights), extent[position] // parts).reshape((-1,) + (1,) * (len(extent) - position - 1))

    factor_of = one(*split[0])
    for cut in split[1:]:
        factor_of = factor_of * one(*cut)
    return factor_of


def split_up(number_of, total, bound, skew):
    portions = [(1 << 20) // math.isqrt(standing ** skew) + 1 for standing in range(2, number_of + 1)]
    surplus, given = total - bound - (number_of - 1), [1] * (number_of - 1)
    while surplus > 0:
        movable = [i for i in range(number_of - 1) if given[i] < bound]
        pool, budget = sum([portions[i] for i in movable]), surplus
        for i in movable:
            addition = min(bound - given[i], max(1, budget * portions[i] // pool), surplus)
            given[i] = given[i] + addition
            surplus = surplus - addition
    return np.array([bound] + given)


def uneven_parts(own_key, amount, total, bound, skew):
    if amount == 2:
        one = jax.random.randint(own_key, (), max(1, total - bound), min(bound, total - 1) + 1)
        return jnp.stack([one, total - one])
    sizes = jnp.asarray(split_up(amount, total, bound, skew), jnp.int32)
    twos = (amount - 1) // 2
    donor, receiver = sizes[1:1 + 2 * twos:2], sizes[2:2 + 2 * twos:2]
    room = jnp.minimum(donor - 1, bound - receiver)
    passed = jax.random.randint(jax.random.fold_in(own_key, 1), (twos,), 0, 1 << 20) % (room + 1)
    sizes = sizes.at[1:1 + 2 * twos:2].set(donor - passed).at[2:2 + 2 * twos:2].set(receiver + passed)
    return sizes[jax.random.permutation(jax.random.fold_in(own_key, 2), amount)]


def normal_values(key, dims, deviation, bound, shards=(), kind=jnp.bfloat16):
    entries = jax.random.normal(key, dims, jnp.float32) * deviation
    if len(shards) > 0:
        entries = level_of(key, dims, shards, -0.22, 0.18) * entries
    return jnp.clip(entries, min=-bound, max=bound).astype(kind)


def setup_inputs(seed: int = 0) -> dict:
    splits = jax.random.split(jax.random.key(seed), 6)
    tokens = draw_tokens(jax.random.fold_in(splits[5], 71), 0)
    kv_weight = draw_kv_weight(jax.random.fold_in(splits[5], 71), 0)
    queries = draw_queries(jax.random.fold_in(splits[5], 71), 0)
    out_grad = normal_values(splits[3], (TOKENS, Q_WIDTH), 1.0, 6.0, ((0, 32),))
    doc_lengths = jax.vmap(lambda own: uneven_parts(own, DOCS, SEQ, DOC_MOST, 2))(jax.random.split(splits[4], GROUPS)).reshape((GROUPS, DOCS)).astype(jnp.int32)
    return {"tokens": tokens, "kv_weight": kv_weight, "queries": queries, "out_grad": out_grad, "doc_lengths": doc_lengths}


NEG_FILL = -1e30


def doc_index(doc_ends, positions):
    return jnp.sum((doc_ends[None, :] <= positions[:, None]).astype(jnp.int32), axis=1).astype(jnp.int32)


def attend(q_rows, kv_window, grad_rows, allowed):
    row_count = q_rows.shape[0]
    group_size = HEADS // KV_HEADS
    inv_root = HEAD_DIM ** -0.5
    out_parts = []
    dq_parts = []
    dk_parts = []
    dv_parts = []
    for head_group in range(KV_HEADS):
        col_start = head_group * group_size * HEAD_DIM
        q_group = q_rows[:, col_start:col_start + group_size * HEAD_DIM].reshape(row_count, group_size, HEAD_DIM).astype(jnp.float32)
        key_block = kv_window[:, head_group * HEAD_DIM:(head_group + 1) * HEAD_DIM].astype(jnp.float32)
        val_start = (KV_HEADS + head_group) * HEAD_DIM
        values = kv_window[:, val_start:val_start + HEAD_DIM].astype(jnp.float32)
        scores = jnp.einsum("qhd,kd->hqk", q_group, key_block) * inv_root
        scores = jnp.where(allowed[None], scores, NEG_FILL)
        row_max = jnp.max(scores, axis=-1, keepdims=True)
        exp_shift = jnp.exp(scores - row_max)
        prob_full = exp_shift / jnp.sum(exp_shift, axis=-1, keepdims=True)
        prob_low = prob_full.astype(jnp.bfloat16)
        out_group = jnp.einsum("hqk,kd->qhd", prob_low.astype(jnp.float32), values).astype(jnp.bfloat16)
        grad_group = grad_rows[:, col_start:col_start + group_size * HEAD_DIM].reshape(row_count, group_size, HEAD_DIM).astype(jnp.float32)
        dprobs = jnp.einsum("qhd,kd->hqk", grad_group, values)
        row_delta = jnp.sum(grad_group * out_group.astype(jnp.float32), axis=-1)
        dscores = (prob_full * (dprobs - row_delta.T[:, :, None])).astype(jnp.bfloat16)
        dq_group = (jnp.einsum("hqk,kd->qhd", dscores.astype(jnp.float32), key_block) * inv_root).astype(jnp.bfloat16)
        dk_group = jnp.einsum("hqk,qhd->kd", dscores.astype(jnp.float32), q_group) * inv_root
        dv_group = jnp.einsum("hqk,qhd->kd", prob_low.astype(jnp.float32), grad_group)
        out_parts.append(out_group.reshape(row_count, group_size * HEAD_DIM))
        dq_parts.append(dq_group.reshape(row_count, group_size * HEAD_DIM))
        dk_parts.append(dk_group)
        dv_parts.append(dv_group)
    return (jnp.concatenate(out_parts, axis=1), jnp.concatenate(dq_parts, axis=1),
            jnp.concatenate(dk_parts + dv_parts, axis=1))


def reference(tokens, kv_weight, queries, out_grad, doc_lengths):
    devices = N_FSDP * N_BAL
    kv_all = jnp.dot(tokens, kv_weight, preferred_element_type=jnp.float32).astype(jnp.bfloat16)
    kv_dev = kv_all.reshape(devices, TOK_DEV, KV_WIDTH)
    q_dev = queries.reshape(devices, TOK_DEV, Q_WIDTH)
    grad_dev = out_grad.reshape(devices, TOK_DEV, Q_WIDTH)
    tok_dev = tokens.reshape(devices, TOK_DEV, D)
    ends_all = jnp.cumsum(doc_lengths, axis=1).astype(jnp.int32)
    row_ids = jnp.arange(TOK_DEV, dtype=jnp.int32)
    zero_kv = jnp.zeros((TOK_DEV, KV_WIDTH), jnp.bfloat16)

    def device_step(pending, dev_index):
        group_id = dev_index // N_BAL
        bal_slot = dev_index % N_BAL
        doc_ends = ends_all[group_id]
        own_pos = (bal_slot * TOK_DEV + row_ids).astype(jnp.int32)
        own_doc = doc_index(doc_ends, own_pos)
        kv_blocks = []
        allowed_parts = []
        for distance in range(REACH, -1, -1):
            key_pos = ((bal_slot - distance) * TOK_DEV + row_ids).astype(jnp.int32)
            key_doc = jnp.where(key_pos >= 0, doc_index(doc_ends, key_pos), -1)
            allowed_parts.append((own_doc[:, None] == key_doc[None, :]) & (key_pos[None, :] <= own_pos[:, None]))
            source = jnp.maximum(dev_index - distance, 0).astype(jnp.int32)
            kv_blocks.append(jnp.where(bal_slot >= distance, kv_dev[source], zero_kv))
        allowed = jnp.concatenate(allowed_parts, axis=1)
        kv_window = jnp.concatenate(kv_blocks, axis=0)
        out_rows, dq_rows, grad_window = attend(q_dev[dev_index], kv_window, grad_dev[dev_index], allowed)
        grad_terms = grad_window.reshape(REACH + 1, TOK_DEV, KV_WIDTH)
        finished = pending[REACH - 1] + grad_terms[REACH]
        new_pending = jnp.concatenate([grad_terms[0:1], pending[:REACH - 1] + grad_terms[1:REACH]], axis=0)
        return new_pending, (out_rows, dq_rows, finished)

    start_pending = jnp.zeros((REACH, TOK_DEV, KV_WIDTH), jnp.float32)
    _, (out_all, dq_all, grad_all) = lax.scan(device_step, start_pending,
                                              jnp.arange(devices, dtype=jnp.int32), reverse=True)
    grad_kv = grad_all.astype(jnp.bfloat16)
    grad_flat = grad_kv.reshape(devices * TOK_DEV, KV_WIDTH)
    grad_tokens = jnp.dot(grad_flat, kv_weight.T, preferred_element_type=jnp.float32).astype(jnp.bfloat16)

    def add_term(running, dev_index):
        term = lax.dot_general(tok_dev[dev_index], grad_kv[dev_index], (((0,), (0,)), ((), ())),
                               preferred_element_type=jnp.float32)
        rounded = lax.optimization_barrier(term.astype(jnp.bfloat16))
        return running + rounded.astype(jnp.float32), None

    grad_weight, _ = lax.scan(add_term, jnp.zeros((D, KV_WIDTH), jnp.float32), jnp.arange(devices, dtype=jnp.int32))
    attn_out = out_all.reshape(devices * TOK_DEV, Q_WIDTH)
    grad_queries = dq_all.reshape(devices * TOK_DEV, Q_WIDTH)
    return attn_out, grad_queries, grad_tokens, grad_weight
```

```python
import functools

import jax
import jax.numpy as jnp
from jax import lax
from jax.experimental import pallas as pl
from jax.experimental.pallas import tpu as pltpu
from jax.sharding import PartitionSpec as P

HEADS = 16
KV_HEADS = 4
HEAD_DIM = 128
REACH = 4

NEG_FILL = -1e30
F32 = jnp.float32
BF16 = jnp.bfloat16
VM = pl.BlockSpec(memory_space=pltpu.VMEM)
SM = pl.BlockSpec(memory_space=pltpu.SMEM)


def swap(value, axis, bit):
    count = lax.axis_size(axis)
    return lax.ppermute(value, axis, [(i, i ^ bit) for i in range(count)])


def dot(a, b, ca, cb):
    return lax.dot_general(a, b, (((ca,), (cb,)), ((), ())), preferred_element_type=F32)


def project_kernel(x0, x1, x2, x3, w_own, w_oth, keep, send):
    for r, x in enumerate((x0, x1, x2, x3)):
        keep[r] = dot(x[...], w_own[...], 1, 0).astype(BF16)
        send[r] = dot(x[...], w_oth[...], 1, 0).astype(BF16)


def project(xs, w_own, w_oth):
    rows = xs[0].shape[0]
    out = jax.ShapeDtypeStruct((4, rows, HEAD_DIM), BF16)
    return pl.pallas_call(
        project_kernel, out_shape=(out, out), in_specs=[VM] * 6, out_specs=(VM, VM)
    )(*xs, w_own, w_oth)


def window_kernel(ids, keep, recv, o0, o1, o2, o3):
    m = ids[0]
    rows = keep.shape[1]
    for r, out in enumerate((o0, o1, o2, o3)):
        target = jnp.bitwise_xor(m, r)
        for w in range(3):
            chip = target + (w - 2)
            ok = chip >= 0
            rel = jnp.bitwise_xor(jnp.maximum(chip, 0), m)
            zero = jnp.zeros((rows, HEAD_DIM), BF16)
            out[2 * w * rows : (2 * w + 1) * rows, :] = jnp.where(ok, keep[rel], zero)
            out[(2 * w + 1) * rows : (2 * w + 2) * rows, :] = jnp.where(ok, recv[rel], zero)


def windows(ids, keep, recv):
    rows = keep.shape[1]
    out = jax.ShapeDtypeStruct((6 * rows, HEAD_DIM), BF16)
    return pl.pallas_call(
        window_kernel, out_shape=(out,) * 4, in_specs=[SM, VM, VM], out_specs=(VM,) * 4
    )(ids, keep, recv)


def attend_kernel(docs, ids, first, second, q_own, q_oth, g_own, g_oth, lens,
                  out_own, out_oth, dq_own, dq_oth, d_first, d_second, bias):
    m, c = ids[0], ids[1]
    rows = q_own.shape[0]
    keys = first.shape[0]
    inv = HEAD_DIM ** (-0.5)

    def place(index, chip0, shape, dim):
        t = lax.broadcasted_iota(jnp.int32, shape, dim)
        chip = t // (2 * rows) + chip0
        within = t % (2 * rows)
        mine = within < rows
        shard = 2 * chip + jnp.where(mine, c, 1 - c)
        return shard * rows + jnp.where(mine, within, within - rows)

    kpos = place(0, m - 2, (keys, 1), 0)
    qpos = place(0, m, (1, 2 * rows), 1)
    kdoc = jnp.where(kpos >= 0, 0, -1)
    qdoc = jnp.zeros_like(qpos)
    end = jnp.int32(0)
    for k in range(docs):
        end = end + lens[0, k]
        kdoc = kdoc + (kpos >= end).astype(jnp.int32)
        qdoc = qdoc + (qpos >= end).astype(jnp.int32)
    bias[...] = jnp.where((kdoc == qdoc) & (kpos <= qpos), 0.0, NEG_FILL)

    is_key = m < 2
    key = jnp.where(is_key, first[...], second[...])
    val = jnp.where(is_key, second[...], first[...])
    key_t = key.T
    val_t = val.T
    dk = jnp.zeros((keys, HEAD_DIM), F32)
    dv = jnp.zeros((keys, HEAD_DIM), F32)
    for h in range(HEADS // KV_HEADS):
        cols = slice(h * HEAD_DIM, (h + 1) * HEAD_DIM)
        q = jnp.concatenate([q_own[:, cols], q_oth[:, cols]], axis=0)
        g = jnp.concatenate([g_own[:, cols], g_oth[:, cols]], axis=0)
        s = dot(key, q, 1, 1) * inv + bias[...]
        p = jnp.exp(s - jnp.max(s, axis=0, keepdims=True))
        p = p * (1.0 / jnp.sum(p, axis=0, keepdims=True))
        low = p.astype(BF16)
        out_t = dot(val_t, low, 1, 0).astype(BF16).astype(F32)
        delta = jnp.sum(out_t * g.astype(F32).T, axis=0, keepdims=True)
        dp = dot(val, g, 1, 1)
        ds = (p * (dp - delta)).astype(BF16)
        dq_t = dot(key_t, ds, 1, 0) * inv
        dk = dk + dot(ds, q, 1, 0)
        dv = dv + dot(low, g, 1, 0)
        out = out_t.T.astype(BF16)
        dq = dq_t.T.astype(BF16)
        out_own[:, cols] = out[:rows]
        out_oth[:, cols] = out[rows:]
        dq_own[:, cols] = dq[:rows]
        dq_oth[:, cols] = dq[rows:]
    dk = (dk * inv).astype(BF16)
    dv = dv.astype(BF16)
    d_first[...] = jnp.where(is_key, dk, dv)
    d_second[...] = jnp.where(is_key, dv, dk)


def attend(first, second, q_own, q_oth, g_own, g_oth, lens, ids):
    rows, width = q_own.shape
    keys = first.shape[0]
    part = jax.ShapeDtypeStruct((rows, width), BF16)
    grad = jax.ShapeDtypeStruct((keys, HEAD_DIM), BF16)
    docs = lens.shape[1]
    return pl.pallas_call(
        functools.partial(attend_kernel, docs),
        out_shape=(part, part, part, part, grad, grad),
        in_specs=[SM] + [VM] * 6 + [SM],
        out_specs=(VM,) * 6,
        scratch_shapes=[pltpu.VMEM((keys, 2 * rows), F32)],
    )(ids, first, second, q_own, q_oth, g_own, g_oth, lens)


def gather_kernel(ids, d0, d1, d2, d3, own, oth, acc):
    m = ids[0]
    rows = own.shape[1]
    acc[...] = jnp.zeros_like(acc)
    for r, d in enumerate((d0, d1, d2, d3)):
        start = pl.multiple_of(jnp.bitwise_xor(m, r) * (2 * rows), 2 * rows)
        span = pl.ds(start, 6 * rows)
        acc[span, :] = acc[span, :] + d[...].astype(F32)
    for r in range(4):
        start = pl.multiple_of((jnp.bitwise_xor(m, r) + 2) * (2 * rows), 2 * rows)
        own[r] = acc[pl.ds(start, rows), :].astype(BF16)
        oth[r] = acc[pl.ds(start + rows, rows), :].astype(BF16)


def gather_grads(ids, ds):
    rows = ds[0].shape[0] // 6
    out = jax.ShapeDtypeStruct((4, rows, HEAD_DIM), BF16)
    return pl.pallas_call(
        gather_kernel,
        out_shape=(out, out),
        in_specs=[SM] + [VM] * 4,
        out_specs=(VM, VM),
        scratch_shapes=[pltpu.VMEM((12 * rows, HEAD_DIM), F32)],
    )(ids, *ds)


def weight_kernel(x0, x1, x2, x3, g_own, g_oth, own, oth):
    for g, out in ((g_own, own), (g_oth, oth)):
        total = None
        for r, x in enumerate((x0, x1, x2, x3)):
            term = dot(g[r].T, x[...], 1, 0)
            total = term if total is None else total + term
        out[...] = total.T.astype(out.dtype)


def weight_grads(xs, g_own, g_oth):
    width = xs[0].shape[1]
    return pl.pallas_call(
        weight_kernel,
        out_shape=(
            jax.ShapeDtypeStruct((width, HEAD_DIM), F32),
            jax.ShapeDtypeStruct((width, HEAD_DIM), BF16),
        ),
        in_specs=[VM] * 6,
        out_specs=(VM, VM),
    )(*xs, g_own, g_oth)


def token_kernel(g_own, g_oth, w_own, w_oth, *outs):
    half = w_own.shape[0] // 2
    for r in range(4):
        g = jnp.concatenate([g_own[r], g_oth[r]], axis=1)
        for part in range(2):
            rows = slice(part * half, (part + 1) * half)
            w = jnp.concatenate([w_own[rows, :], w_oth[rows, :]], axis=1)
            outs[2 * r + part][...] = dot(g, w, 1, 1).astype(BF16)


def token_grads(g_own, g_oth, w_own, w_oth):
    rows, half = g_own.shape[1], w_own.shape[0] // 2
    return pl.pallas_call(
        token_kernel,
        out_shape=(jax.ShapeDtypeStruct((rows, half), BF16),) * 8,
        in_specs=[VM] * 4,
        out_specs=(VM,) * 8,
    )(g_own, g_oth, w_own, w_oth)


def assemble_kernel(ids, *refs):
    m, c = ids[0], ids[1]
    out = refs[-1]
    for side in range(2):
        core = c if side == 0 else 1 - c
        for r in range(4):
            q = jnp.bitwise_xor(m, r)
            col = (q // 2) * (KV_HEADS * HEAD_DIM) + (2 * core + q % 2) * HEAD_DIM
            col = pl.multiple_of(col, HEAD_DIM)
            out[:, pl.ds(col, HEAD_DIM)] = refs[4 * side + r][...].astype(F32)


def assemble(ids, blocks):
    rows = blocks[0].shape[0]
    return pl.pallas_call(
        assemble_kernel,
        out_shape=jax.ShapeDtypeStruct((rows, 2 * KV_HEADS * HEAD_DIM), F32),
        in_specs=[SM] + [VM] * 8,
        out_specs=VM,
    )(ids, *blocks)


def plane_local(tokens, kv_weight, queries, out_grad, doc_lengths):
    half = queries.shape[1] // 2
    rows = tokens.shape[0]
    b = lax.axis_index("bal")
    z = lax.axis_index("fsdp")
    m, c = b // 2, b % 2
    ids = jnp.stack([m, c]).astype(jnp.int32)
    pair = lambda v: swap(v, "bal", 1)
    near = lambda v: swap(v, "bal", 2)
    far = lambda v: swap(v, "bal", 4)
    cross = lambda v: swap(v, "bal", 6)

    col = (m // 2) * (KV_HEADS * HEAD_DIM) + (2 * c + m % 2) * HEAD_DIM
    w0 = lax.dynamic_slice(kv_weight, (0, col), (kv_weight.shape[0], HEAD_DIM))
    w2 = swap(w0, "fsdp", 2)
    w13 = swap(jnp.stack([w0, w2]), "fsdp", 1)
    blocks = jnp.stack([w0, w13[0], w2, w13[1]])
    w_own = jnp.take(blocks, jnp.arange(4) ^ z, axis=0).reshape(-1, HEAD_DIM)
    w_oth = pair(w_own)

    xs = [tokens, near(tokens), far(tokens), cross(tokens)]

    q_own = lax.dynamic_slice(queries, (0, c * half), (rows, half))
    g_own = lax.dynamic_slice(out_grad, (0, c * half), (rows, half))
    q_oth = pair(lax.dynamic_slice(queries, (0, (1 - c) * half), (rows, half)))
    g_oth = pair(lax.dynamic_slice(out_grad, (0, (1 - c) * half), (rows, half)))

    keep, send = project(xs, w_own, w_oth)
    win = windows(ids, keep, pair(send))
    win_x, win_y, win_d = near(win[1]), far(win[2]), cross(win[3])

    width = half // 2
    ga, gb = m % 2, 1 - m % 2
    cut = lambda v, g: lax.dynamic_slice(v, (0, g * width), (rows, width))
    oa = attend(win[0], win_y, *[cut(v, ga) for v in (q_own, q_oth, g_own, g_oth)], doc_lengths, ids)
    ob = attend(win_x, win_d, *[cut(v, gb) for v in (q_own, q_oth, g_own, g_oth)], doc_lengths, ids)

    grads = [oa[4], near(ob[4]), far(oa[5]), cross(ob[5])]
    g_keep, g_send = gather_grads(ids, grads)
    g_recv = pair(g_send)

    w_mine, w_send = weight_grads(xs, g_keep, g_recv)
    total = w_mine + pair(w_send).astype(F32)
    total = total.reshape(4, -1, HEAD_DIM)
    rel = jnp.take(total, jnp.arange(4) ^ z, axis=0)
    got = swap(rel[1::2].astype(BF16), "fsdp", 1).astype(F32)
    a0, a2 = rel[0] + got[0], rel[2] + got[1]
    block = (a0 + swap(a2.astype(BF16), "fsdp", 2).astype(F32)).astype(BF16)
    mine = [block, near(block), far(block), cross(block)]
    theirs = [pair(v) for v in mine]
    grad_weight = assemble(ids, mine + theirs)

    t = token_grads(g_keep, g_recv, w_own, w_oth)
    t = [v.astype(F32) for v in t]
    send_a = near(jnp.concatenate([t[2], t[6]], axis=0).astype(BF16)).astype(F32)
    send_b = far(jnp.concatenate([t[5], t[7]], axis=0).astype(BF16)).astype(F32)
    a0, a2 = t[0] + send_a[:rows], t[4] + send_a[rows:]
    b0, b1 = t[1] + send_b[:rows], t[3] + send_b[rows:]
    a0 = a0 + far(a2.astype(BF16)).astype(F32)
    b0 = b0 + near(b1.astype(BF16)).astype(F32)
    grad_tokens = jnp.concatenate([a0, b0], axis=1).astype(BF16)

    def place(own_a, own_b, oth_a, oth_b):
        order = lambda a, b_: jnp.where(ga == 0, jnp.concatenate([a, b_], 1), jnp.concatenate([b_, a], 1))
        own = order(own_a, own_b)
        got = pair(order(oth_a, oth_b))
        return jnp.where(c == 0, jnp.concatenate([own, got], 1), jnp.concatenate([got, own], 1))

    attn_out = place(oa[0], ob[0], oa[1], ob[1])
    grad_queries = place(oa[2], ob[2], oa[3], ob[3])
    return attn_out, grad_queries, grad_tokens, grad_weight


def from_behind(value, axis, steps):
    count = lax.axis_size(axis)
    initial, last = (max(0, -steps), min(count, count - steps))
    return lax.ppermute(value, axis, [(source, source + steps) for source in range(initial, last)])


def doc_index(doc_ends, positions):
    return jnp.sum((doc_ends[None, :] <= positions[:, None]).astype(jnp.int32), axis=1)


def score_tile(q_group, key_block, mask_block, inv_root):
    raw_scores = (
        jnp.einsum("qhd,kd->hqk", q_group, key_block, preferred_element_type=jnp.float32) * inv_root
    )
    return jnp.where(mask_block[None], raw_scores, NEG_FILL)


def value_tile(prob_tile, value_block):
    return jnp.einsum("hqk,kd->qhd", prob_tile, value_block, preferred_element_type=jnp.float32)


def dprob_tile(grad_group, value_block):
    return jnp.einsum("qhd,kd->hqk", grad_group, value_block, preferred_element_type=jnp.float32)


def query_tile(dscore_tile, key_block):
    return jnp.einsum("hqk,kd->qhd", dscore_tile, key_block, preferred_element_type=jnp.float32)


def key_tile(dscore_tile, q_group, inv_root):
    return (
        jnp.einsum("hqk,qhd->kd", dscore_tile, q_group, preferred_element_type=jnp.float32)
        * inv_root
    )


def value_grad_tile(prob_tile, grad_group):
    return jnp.einsum("hqk,qhd->kd", prob_tile, grad_group, preferred_element_type=jnp.float32)


def attend_rows(q_rows, kv_blocks, grad_rows, allowed_parts):
    row_count = q_rows.shape[0]
    key_rows = kv_blocks[0].shape[0]
    group_size = HEADS // KV_HEADS
    inv_root = HEAD_DIM ** (-0.5)
    window_range = list(range(len(kv_blocks)))
    row_shape = (row_count, group_size, HEAD_DIM)
    out_parts = []
    dq_parts = []
    key_grads = [[] for window_pos in window_range]
    value_grads = [[] for window_pos in window_range]
    for head_group in range(KV_HEADS):
        col_start = head_group * group_size * HEAD_DIM
        col_stop = col_start + group_size * HEAD_DIM
        val_start = (KV_HEADS + head_group) * HEAD_DIM
        q_group = q_rows[:, col_start:col_stop].reshape(row_shape)
        grad_group = grad_rows[:, col_start:col_stop].reshape(row_shape)
        key_list = [
            piece[:, head_group * HEAD_DIM : (head_group + 1) * HEAD_DIM] for piece in kv_blocks
        ]
        value_list = [piece[:, val_start : val_start + HEAD_DIM] for piece in kv_blocks]
        score_tiles = [
            score_tile(q_group, key_list[window_pos], allowed_parts[window_pos], inv_root)
            for window_pos in window_range
        ]
        scores = jnp.concatenate(score_tiles, axis=2)
        row_max = jnp.max(scores, axis=-1, keepdims=True)
        exp_shift = jnp.exp(scores - row_max)
        prob_full = exp_shift / jnp.sum(exp_shift, axis=-1, keepdims=True)
        prob_low = prob_full.astype(jnp.bfloat16)
        prob_tiles = [
            prob_low[:, :, window_pos * key_rows : (window_pos + 1) * key_rows]
            for window_pos in window_range
        ]
        out_accum = jnp.zeros(row_shape, jnp.float32)
        for window_pos in window_range:
            out_accum = out_accum + value_tile(prob_tiles[window_pos], value_list[window_pos])
        out_group = out_accum.astype(jnp.bfloat16)
        row_delta = jnp.sum(grad_group.astype(jnp.float32) * out_group.astype(jnp.float32), axis=-1)
        dprob_tiles = [
            dprob_tile(grad_group, value_list[window_pos]) for window_pos in window_range
        ]
        dprobs = jnp.concatenate(dprob_tiles, axis=2)
        dscores = (prob_full * (dprobs - row_delta.T[:, :, None])).astype(jnp.bfloat16)
        dq_accum = jnp.zeros(row_shape, jnp.float32)
        for window_pos in window_range:
            dscore_piece = dscores[:, :, window_pos * key_rows : (window_pos + 1) * key_rows]
            dq_accum = dq_accum + query_tile(dscore_piece, key_list[window_pos])
            key_grads[window_pos].append(key_tile(dscore_piece, q_group, inv_root))
            value_grads[window_pos].append(value_grad_tile(prob_tiles[window_pos], grad_group))
        dq_group = (dq_accum * inv_root).astype(jnp.bfloat16)
        out_parts.append(out_group.reshape(row_count, group_size * HEAD_DIM))
        dq_parts.append(dq_group.reshape(row_count, group_size * HEAD_DIM))
    window_terms = [
        jnp.concatenate(key_grads[window_pos] + value_grads[window_pos], axis=1)
        for window_pos in window_range
    ]
    return (jnp.concatenate(out_parts, axis=1), jnp.concatenate(dq_parts, axis=1), window_terms)


def local(tokens, kv_weight, queries, out_grad, doc_lengths):
    row_count = tokens.shape[0]
    bal_index = lax.axis_index("bal")
    doc_ends = jnp.cumsum(doc_lengths[0])
    row_ids = jnp.arange(row_count, dtype=jnp.int32)
    own_pos = bal_index * row_count + row_ids
    own_doc = doc_index(doc_ends, own_pos)
    allowed_parts = []
    for distance in range(REACH, -1, -1):
        key_pos = (bal_index - distance) * row_count + row_ids
        key_doc = jnp.where(key_pos >= 0, doc_index(doc_ends, key_pos), -1)
        allowed_parts.append(
            (own_doc[:, None] == key_doc[None, :]) & (key_pos[None, :] <= own_pos[:, None])
        )
    full_weight = lax.all_gather(kv_weight, "fsdp", axis=0, tiled=True)
    kv_accum = jnp.dot(tokens, full_weight, preferred_element_type=jnp.float32)
    kv_rows = kv_accum.astype(jnp.bfloat16)
    earlier = [kv_rows]
    for distance in range(1, REACH + 1):
        earlier.append(from_behind(kv_rows, "bal", distance))
    kv_blocks = earlier[::-1]
    attn_out, grad_queries, window_terms = attend_rows(queries, kv_blocks, out_grad, allowed_parts)
    grad_terms = window_terms[::-1]
    grad_sum = grad_terms[0]
    for distance in range(1, REACH + 1):
        grad_sum = grad_sum + from_behind(
            grad_terms[distance].astype(jnp.bfloat16), "bal", -distance
        ).astype(jnp.float32)
    grad_kv = grad_sum.astype(jnp.bfloat16)
    grad_tokens = lax.dot_general(
        grad_kv, full_weight, (((1,), (1,)), ((), ())), preferred_element_type=jnp.float32
    ).astype(jnp.bfloat16)
    shard_sum = lax.psum_scatter(
        lax.dot_general(
            tokens, grad_kv, (((0,), (0,)), ((), ())), preferred_element_type=jnp.float32
        ).astype(jnp.bfloat16),
        "fsdp",
        scatter_dimension=0,
        tiled=True,
    )
    grad_weight = lax.psum(shard_sum, "bal").astype(jnp.float32)
    return (attn_out, grad_queries, grad_tokens, grad_weight)


def solution(mesh):
    placed = (
        P(("fsdp", "bal"), None),
        P("fsdp", None),
        P(("fsdp", "bal"), None),
        P(("fsdp", "bal"), None),
        P("fsdp", None),
    )
    one_plane = mesh.shape["bal"] == 8 and mesh.shape["fsdp"] == 4
    return jax.shard_map(
        plane_local if one_plane else local,
        mesh=mesh,
        in_specs=placed,
        out_specs=(
            P(("fsdp", "bal"), None),
            P(("fsdp", "bal"), None),
            P(("fsdp", "bal"), None),
            P("fsdp", None),
        ),
        check_vma=False,
    )
```

```python
import functools

import jax
import jax.numpy as jnp
from jax import lax
from jax.experimental import pallas as pl
from jax.experimental.pallas import tpu as pltpu
from jax.sharding import PartitionSpec as P

HEADS = 16
KV_HEADS = 4
HEAD_DIM = 128
REACH = 4

NEG_FILL = -1e30
F32 = jnp.float32
BF16 = jnp.bfloat16


def swap(value, axis, bit):
    count = lax.axis_size(axis)
    return lax.ppermute(value, axis, [(i, i ^ bit) for i in range(count)])


def dot(a, b, ca, cb):
    return lax.dot_general(a, b, (((ca,), (cb,)), ((), ())), preferred_element_type=F32)


def on_chip(shape, dtype=BF16):
    return pltpu.VMEM(shape, dtype)


def run(body, outs, scalars, arrays, scratch=(), room=16):
    arrays = [pltpu.with_memory_space_constraint(v, pltpu.VMEM) for v in arrays]
    return pl.pallas_call(
        body,
        out_shape=outs,
        in_specs=[pl.BlockSpec(memory_space=pltpu.SMEM)] * len(scalars)
        + [pl.BlockSpec(memory_space=pltpu.VMEM)] * len(arrays),
        out_specs=jax.tree.map(
            lambda _: pl.BlockSpec(memory_space=pltpu.VMEM), outs, is_leaf=lambda v: hasattr(v, "dtype")
        ),
        scratch_shapes=scratch,
        compiler_params=pltpu.CompilerParams(vmem_limit_bytes=room << 20),
    )(*scalars, *arrays)


def head_of(chip):
    return jnp.bitwise_xor(chip % 2, chip // 2)


def column_of(chip, core):
    return (chip // 2) * (KV_HEADS * HEAD_DIM) + (2 * core + head_of(chip)) * HEAD_DIM


def quarter(z, r, size):
    return pl.ds(pl.multiple_of(jnp.bitwise_xor(z, r) * size, size), size)


def project_rows(z, xs, ws):
    size = ws[0].shape[0]
    total = None
    for r, w in enumerate(ws):
        x = jnp.concatenate([x[:, quarter(z, r, size)] for x in xs], axis=0)
        term = dot(x, w, 1, 0)
        total = term if total is None else total + term
    return total.astype(BF16)


def project_kernel(ids, *refs):
    *xs, w0, w2, w13, out = refs
    ws = (w0[...], w13[0], w2[...], w13[1])
    out[...] = project_rows(ids[2], xs, ws)


def window_kernel(ids, *refs):
    *xs, w0, w2, w13, first, o0, o1, o2, o3, kv = refs
    ws = (w0[...], w13[0], w2[...], w13[1])
    m = ids[0]
    rows = first.shape[0] // 3
    for r in range(3):
        kv[r] = first[r * rows : (r + 1) * rows, :]
    kv[3] = project_rows(ids[2], xs, ws)
    for r, out in ((3, o3), (1, o1), (2, o2), (0, o0)):
        target = jnp.bitwise_xor(m, r)
        for w in range(3):
            chip = target + (w - 2)
            rel = jnp.bitwise_xor(jnp.maximum(chip, 0), m)
            out[w * rows : (w + 1) * rows, :] = jnp.where(
                chip >= 0, kv[rel], jnp.zeros((rows, HEAD_DIM), BF16)
            )


def attend_kernel(side, docs, ids, lens, first, second, q_own, q_oth, g_own, g_oth,
                  own, oth, d_first, d_second, bias):
    m, c = ids[0], ids[1]
    rows = q_own.shape[0]
    keys = first.shape[0]
    inv = HEAD_DIM ** (-0.5)
    heads = HEADS // KV_HEADS
    head = head_of(m) if side == 0 else 1 - head_of(m)
    base = (2 * c + head) * (heads * HEAD_DIM)

    def place(chip0, shape, dim):
        t = lax.broadcasted_iota(jnp.int32, shape, dim)
        chip = t // (2 * rows) + chip0
        within = t % (2 * rows)
        mine = within < rows
        shard = 2 * chip + jnp.where(mine, c, 1 - c)
        return shard * rows + jnp.where(mine, within, within - rows)

    kpos = place(m - 2, (keys, 1), 0)
    qpos = place(m, (1, 2 * rows), 1)
    kdoc = jnp.where(kpos >= 0, 0, -1)
    qdoc = jnp.zeros_like(qpos)
    end = jnp.int32(0)
    for k in range(docs):
        end = end + lens[0, k]
        kdoc = kdoc + (kpos >= end).astype(jnp.int32)
        qdoc = qdoc + (qpos >= end).astype(jnp.int32)
    bias[...] = jnp.where((kdoc == qdoc) & (kpos <= qpos), 0.0, NEG_FILL)

    is_key = m < 2
    key = jnp.where(is_key, first[...], second[...])
    val = jnp.where(is_key, second[...], first[...])
    key_t = key.T
    val_t = val.T
    dk = jnp.zeros((keys, HEAD_DIM), F32)
    dv = jnp.zeros((keys, HEAD_DIM), F32)
    for h in range(heads):
        cols = pl.ds(pl.multiple_of(base + h * HEAD_DIM, HEAD_DIM), HEAD_DIM)
        q = jnp.concatenate([q_own[:, cols], q_oth[:, cols]], axis=0)
        g = jnp.concatenate([g_own[:, cols], g_oth[:, cols]], axis=0)
        s = dot(key, q, 1, 1) * inv + bias[...]
        p = jnp.exp(s - jnp.max(s, axis=0, keepdims=True))
        p = p * (1.0 / jnp.sum(p, axis=0, keepdims=True))
        low = p.astype(BF16)
        out_t = dot(val_t, low, 1, 0).astype(BF16).astype(F32)
        delta = jnp.sum(out_t * g.astype(F32).T, axis=0, keepdims=True)
        dp = dot(val, g, 1, 1)
        ds = (p * (dp - delta)).astype(BF16)
        dq_t = dot(key_t, ds, 1, 0) * inv
        dk = dk + dot(ds, q, 1, 0)
        dv = dv + dot(low, g, 1, 0)
        out = out_t.T.astype(BF16)
        dq = dq_t.T.astype(BF16)
        at = slice(h * HEAD_DIM, (h + 1) * HEAD_DIM)
        own[0, :, at] = out[:rows]
        oth[0, :, at] = out[rows:]
        own[1, :, at] = dq[:rows]
        oth[1, :, at] = dq[rows:]
    dk = (dk * inv).astype(BF16)
    dv = dv.astype(BF16)
    d_first[...] = jnp.where(is_key, dk, dv)
    d_second[...] = jnp.where(is_key, dv, dk)


def attend(side, ids, lens, first, second, rest):
    rows = rest[0].shape[0]
    keys = first.shape[0]
    part = on_chip((2, rows, HEADS // KV_HEADS * HEAD_DIM))
    grad = on_chip((keys, HEAD_DIM))
    return run(
        functools.partial(attend_kernel, side, lens.shape[1]),
        (part, part, grad, grad),
        (ids, lens),
        (first, second, *rest),
        scratch=[pltpu.VMEM((keys, 2 * rows), F32)],
        room=24,
    )


def place_kernel(ids, own_a, own_b, got_a, got_b, out, dq):
    m, c = ids[0], ids[1]
    width = own_a.shape[2]
    for ref, core, head in (
        (own_a, c, head_of(m)),
        (own_b, c, 1 - head_of(m)),
        (got_a, 1 - c, head_of(m)),
        (got_b, 1 - c, 1 - head_of(m)),
    ):
        cols = pl.ds(pl.multiple_of((2 * core + head) * width, width), width)
        out[:, cols] = ref[0]
        dq[:, cols] = ref[1]


def weight_block(z, r, g_t, xs, size):
    x = jnp.concatenate([x[:, quarter(z, r, size)] for x in xs], axis=0)
    return dot(g_t, x, 1, 0).T


def sum_kernel(ids, *refs):
    d0, d1, d2, d3, *xs, own, oth, g_t, send, acc = refs
    m, z = ids[0], ids[2]
    rows = own.shape[1]
    acc[...] = jnp.zeros_like(acc)
    for r, d in enumerate((d0, d1, d2, d3)):
        start = pl.multiple_of(jnp.bitwise_xor(m, r) * (2 * rows), 2 * rows)
        span = pl.ds(start, 6 * rows)
        acc[span, :] = acc[span, :] + d[...].astype(F32)
    for r in range(4):
        start = pl.multiple_of((jnp.bitwise_xor(m, r) + 2) * (2 * rows), 2 * rows)
        g = acc[pl.ds(start, 2 * rows), :].astype(BF16)
        own[r] = g[:rows]
        oth[r] = g[rows:]
        g_t[:, r * 2 * rows : (r + 1) * 2 * rows] = g.T
    for i, r in enumerate((1, 3)):
        send[i] = weight_block(z, r, g_t[...], xs, send.shape[1]).astype(BF16)


def keep_kernel(ids, g_t, *refs):
    *xs, keep = refs
    for i, r in enumerate((0, 2)):
        keep[i] = weight_block(ids[2], r, g_t[...], xs, keep.shape[1])


def fold_kernel(keep, got, now, later):
    now[...] = keep[0] + got[0].astype(F32)
    later[...] = (keep[1] + got[1].astype(F32)).astype(BF16)


def last_kernel(now, got, out):
    out[...] = (now[...] + got[...].astype(F32)).astype(BF16)


def assemble_kernel(ids, *refs):
    m, c = ids[0], ids[1]
    out = refs[-1]
    for side in range(2):
        core = c if side == 0 else 1 - c
        for r in range(4):
            col = pl.multiple_of(column_of(jnp.bitwise_xor(m, r), core), HEAD_DIM)
            out[:, pl.ds(col, HEAD_DIM)] = refs[4 * side + r][...].astype(F32)


def token_kernel(own, oth, w0, w2, w13, u0, u2, u13, send_a, send_b, keep_a, keep_b):
    rows = own.shape[1]
    g = jnp.concatenate(
        [jnp.concatenate([own[r] for r in range(4)], axis=0),
         jnp.concatenate([oth[r] for r in range(4)], axis=0)], axis=1)
    ws = (w0[...], w13[0], w2[...], w13[1])
    us = (u0[...], u13[0], u2[...], u13[1])
    size = w0.shape[0]
    for i in range(4):
        w = jnp.concatenate([ws[i], us[i]], axis=1)
        t = dot(g, w, 1, 1)
        at = slice((i % 2) * size, (i % 2 + 1) * size)
        send, keep, away = (send_a, keep_a, (1, 3)) if i < 2 else (send_b, keep_b, (2, 3))
        home = [r for r in range(4) if r not in away]
        for k in range(2):
            send[k, :, at] = t[away[k] * rows : (away[k] + 1) * rows].astype(BF16)
            keep[k, :, at] = t[home[k] * rows : (home[k] + 1) * rows]


def fold_both_kernel(keep_a, got_a, keep_b, got_b, a, a_send, b, b_send):
    fold_kernel(keep_a, got_a, a, a_send)
    fold_kernel(keep_b, got_b, b, b_send)


def token_last_kernel(ids, a, got_a, b, got_b, out):
    size = out.shape[1] // 4
    for i in range(4):
        now, got = (a, got_a) if i < 2 else (b, got_b)
        at = slice((i % 2) * size, (i % 2 + 1) * size)
        out[:, quarter(ids[2], i, size)] = (now[:, at] + got[:, at].astype(F32)).astype(BF16)


def plane_local(tokens, kv_weight, queries, out_grad, doc_lengths):
    rows, width = tokens.shape
    size = kv_weight.shape[0]
    m, c = lax.axis_index("bal") // 2, lax.axis_index("bal") % 2
    ids = jnp.stack([m, c, lax.axis_index("fsdp")]).astype(jnp.int32)
    pair = lambda v: swap(v, "bal", 1)
    near = lambda v: swap(v, "bal", 2)
    far = lambda v: swap(v, "bal", 4)
    cross = lambda v: swap(v, "bal", 6)

    x1, x2 = near(tokens), far(tokens)
    w0 = lax.dynamic_slice(kv_weight, (0, column_of(m, c)), (size, HEAD_DIM))
    w2 = swap(w0, "fsdp", 2)
    w13 = swap(jnp.stack([w0, w2]), "fsdp", 1)
    ws = (w0, w2, w13)
    x3 = (far(x1[: rows // 2]), near(x2[rows // 2 :]))
    y0, y1, y2 = pair(tokens), pair(x1), pair(x2)
    y3 = (pair(x3[0]), pair(x3[1]))
    early = (tokens, y0, x1, y1, x2, y2)
    late = (*x3, *y3)
    xs = early + late

    rest = (queries, pair(queries), out_grad, pair(out_grad))

    first = run(project_kernel, on_chip((6 * rows, HEAD_DIM)), (ids,), early + ws)
    win = run(
        window_kernel,
        (on_chip((6 * rows, HEAD_DIM)),) * 4,
        (ids,),
        late + ws + (first,),
        scratch=[pltpu.VMEM((4, 2 * rows, HEAD_DIM), BF16)],
    )
    win3, win1, win2 = cross(win[3]), near(win[1]), far(win[2])

    own_a, oth_a, d0, d3 = attend(0, ids, doc_lengths, win[0], win3, rest)
    d3 = cross(d3)
    own_b, oth_b, d1, d2 = attend(1, ids, doc_lengths, win1, win2, rest)
    d1, d2 = near(d1), far(d2)

    block = on_chip((4, rows, HEAD_DIM))
    g_own, g_oth, g_t, send = run(
        sum_kernel,
        (block, block, on_chip((HEAD_DIM, 8 * rows)), on_chip((2, size, HEAD_DIM))),
        (ids,),
        (d0, d1, d2, d3) + xs,
        scratch=[pltpu.VMEM((12 * rows, HEAD_DIM), F32)],
    )
    got = swap(send, "fsdp", 1)
    g_oth = pair(g_oth)
    keep = run(keep_kernel, on_chip((2, size, HEAD_DIM), F32), (ids,), (g_t,) + xs)
    us = tuple(pair(v) for v in ws)
    half = (rows, width // 2)
    send_a, send_b, keep_a, keep_b = run(
        token_kernel,
        (on_chip((2, *half)), on_chip((2, *half)), on_chip((2, *half), F32), on_chip((2, *half), F32)),
        (),
        (g_own, g_oth) + ws + us,
    )
    got_a, got_b = near(send_a), far(send_b)
    fold = (on_chip((size, HEAD_DIM), F32), on_chip((size, HEAD_DIM)))
    now, later = run(fold_kernel, fold, (), (keep, got))
    got = swap(later, "fsdp", 2)
    fold = (on_chip(half, F32), on_chip(half))
    a, a_send, b, b_send = run(fold_both_kernel, fold + fold, (), (keep_a, got_a, keep_b, got_b))
    got_a, got_b = far(a_send), near(b_send)
    mine = run(last_kernel, on_chip((size, HEAD_DIM)), (), (now, got))
    mine = [mine, near(mine), far(mine), cross(mine)]
    theirs = [pair(v) for v in mine]
    grad_weight = run(
        assemble_kernel,
        jax.ShapeDtypeStruct((size, kv_weight.shape[1]), F32),
        (ids,),
        mine + theirs,
    )
    grad_tokens = run(
        token_last_kernel, jax.ShapeDtypeStruct(tokens.shape, BF16), (ids,), (a, got_a, b, got_b)
    )
    like = jax.ShapeDtypeStruct(queries.shape, BF16)
    attn_out, grad_queries = run(
        place_kernel, (like, like), (ids,), (own_a, own_b, pair(oth_a), pair(oth_b))
    )
    return attn_out, grad_queries, grad_tokens, grad_weight


def from_behind(value, axis, steps):
    count = lax.axis_size(axis)
    initial, last = (max(0, -steps), min(count, count - steps))
    return lax.ppermute(value, axis, [(source, source + steps) for source in range(initial, last)])


def doc_index(doc_ends, positions):
    return jnp.sum((doc_ends[None, :] <= positions[:, None]).astype(jnp.int32), axis=1)


def score_tile(q_group, key_block, mask_block, inv_root):
    raw_scores = (
        jnp.einsum("qhd,kd->hqk", q_group, key_block, preferred_element_type=jnp.float32) * inv_root
    )
    return jnp.where(mask_block[None], raw_scores, NEG_FILL)


def value_tile(prob_tile, value_block):
    return jnp.einsum("hqk,kd->qhd", prob_tile, value_block, preferred_element_type=jnp.float32)


def dprob_tile(grad_group, value_block):
    return jnp.einsum("qhd,kd->hqk", grad_group, value_block, preferred_element_type=jnp.float32)


def query_tile(dscore_tile, key_block):
    return jnp.einsum("hqk,kd->qhd", dscore_tile, key_block, preferred_element_type=jnp.float32)


def key_tile(dscore_tile, q_group, inv_root):
    return (
        jnp.einsum("hqk,qhd->kd", dscore_tile, q_group, preferred_element_type=jnp.float32)
        * inv_root
    )


def value_grad_tile(prob_tile, grad_group):
    return jnp.einsum("hqk,qhd->kd", prob_tile, grad_group, preferred_element_type=jnp.float32)


def attend_rows(q_rows, kv_blocks, grad_rows, allowed_parts):
    row_count = q_rows.shape[0]
    key_rows = kv_blocks[0].shape[0]
    group_size = HEADS // KV_HEADS
    inv_root = HEAD_DIM ** (-0.5)
    window_range = list(range(len(kv_blocks)))
    row_shape = (row_count, group_size, HEAD_DIM)
    out_parts = []
    dq_parts = []
    key_grads = [[] for window_pos in window_range]
    value_grads = [[] for window_pos in window_range]
    for head_group in range(KV_HEADS):
        col_start = head_group * group_size * HEAD_DIM
        col_stop = col_start + group_size * HEAD_DIM
        val_start = (KV_HEADS + head_group) * HEAD_DIM
        q_group = q_rows[:, col_start:col_stop].reshape(row_shape)
        grad_group = grad_rows[:, col_start:col_stop].reshape(row_shape)
        key_list = [
            piece[:, head_group * HEAD_DIM : (head_group + 1) * HEAD_DIM] for piece in kv_blocks
        ]
        value_list = [piece[:, val_start : val_start + HEAD_DIM] for piece in kv_blocks]
        score_tiles = [
            score_tile(q_group, key_list[window_pos], allowed_parts[window_pos], inv_root)
            for window_pos in window_range
        ]
        scores = jnp.concatenate(score_tiles, axis=2)
        row_max = jnp.max(scores, axis=-1, keepdims=True)
        exp_shift = jnp.exp(scores - row_max)
        prob_full = exp_shift / jnp.sum(exp_shift, axis=-1, keepdims=True)
        prob_low = prob_full.astype(jnp.bfloat16)
        prob_tiles = [
            prob_low[:, :, window_pos * key_rows : (window_pos + 1) * key_rows]
            for window_pos in window_range
        ]
        out_accum = jnp.zeros(row_shape, jnp.float32)
        for window_pos in window_range:
            out_accum = out_accum + value_tile(prob_tiles[window_pos], value_list[window_pos])
        out_group = out_accum.astype(jnp.bfloat16)
        row_delta = jnp.sum(grad_group.astype(jnp.float32) * out_group.astype(jnp.float32), axis=-1)
        dprob_tiles = [
            dprob_tile(grad_group, value_list[window_pos]) for window_pos in window_range
        ]
        dprobs = jnp.concatenate(dprob_tiles, axis=2)
        dscores = (prob_full * (dprobs - row_delta.T[:, :, None])).astype(jnp.bfloat16)
        dq_accum = jnp.zeros(row_shape, jnp.float32)
        for window_pos in window_range:
            dscore_piece = dscores[:, :, window_pos * key_rows : (window_pos + 1) * key_rows]
            dq_accum = dq_accum + query_tile(dscore_piece, key_list[window_pos])
            key_grads[window_pos].append(key_tile(dscore_piece, q_group, inv_root))
            value_grads[window_pos].append(value_grad_tile(prob_tiles[window_pos], grad_group))
        dq_group = (dq_accum * inv_root).astype(jnp.bfloat16)
        out_parts.append(out_group.reshape(row_count, group_size * HEAD_DIM))
        dq_parts.append(dq_group.reshape(row_count, group_size * HEAD_DIM))
    window_terms = [
        jnp.concatenate(key_grads[window_pos] + value_grads[window_pos], axis=1)
        for window_pos in window_range
    ]
    return (jnp.concatenate(out_parts, axis=1), jnp.concatenate(dq_parts, axis=1), window_terms)


def local(tokens, kv_weight, queries, out_grad, doc_lengths):
    row_count = tokens.shape[0]
    bal_index = lax.axis_index("bal")
    doc_ends = jnp.cumsum(doc_lengths[0])
    row_ids = jnp.arange(row_count, dtype=jnp.int32)
    own_pos = bal_index * row_count + row_ids
    own_doc = doc_index(doc_ends, own_pos)
    allowed_parts = []
    for distance in range(REACH, -1, -1):
        key_pos = (bal_index - distance) * row_count + row_ids
        key_doc = jnp.where(key_pos >= 0, doc_index(doc_ends, key_pos), -1)
        allowed_parts.append(
            (own_doc[:, None] == key_doc[None, :]) & (key_pos[None, :] <= own_pos[:, None])
        )
    full_weight = lax.all_gather(kv_weight, "fsdp", axis=0, tiled=True)
    kv_accum = jnp.dot(tokens, full_weight, preferred_element_type=jnp.float32)
    kv_rows = kv_accum.astype(jnp.bfloat16)
    earlier = [kv_rows]
    for distance in range(1, REACH + 1):
        earlier.append(from_behind(kv_rows, "bal", distance))
    kv_blocks = earlier[::-1]
    attn_out, grad_queries, window_terms = attend_rows(queries, kv_blocks, out_grad, allowed_parts)
    grad_terms = window_terms[::-1]
    grad_sum = grad_terms[0]
    for distance in range(1, REACH + 1):
        grad_sum = grad_sum + from_behind(
            grad_terms[distance].astype(jnp.bfloat16), "bal", -distance
        ).astype(jnp.float32)
    grad_kv = grad_sum.astype(jnp.bfloat16)
    grad_tokens = lax.dot_general(
        grad_kv, full_weight, (((1,), (1,)), ((), ())), preferred_element_type=jnp.float32
    ).astype(jnp.bfloat16)
    shard_sum = lax.psum_scatter(
        lax.dot_general(
            tokens, grad_kv, (((0,), (0,)), ((), ())), preferred_element_type=jnp.float32
        ).astype(jnp.bfloat16),
        "fsdp",
        scatter_dimension=0,
        tiled=True,
    )
    grad_weight = lax.psum(shard_sum, "bal").astype(jnp.float32)
    return (attn_out, grad_queries, grad_tokens, grad_weight)


def solution(mesh):
    placed = (
        P(("fsdp", "bal"), None),
        P("fsdp", None),
        P(("fsdp", "bal"), None),
        P(("fsdp", "bal"), None),
        P("fsdp", None),
    )
    one_plane = mesh.shape["bal"] == 8 and mesh.shape["fsdp"] == 4
    return jax.shard_map(
        plane_local if one_plane else local,
        mesh=mesh,
        in_specs=placed,
        out_specs=(
            P(("fsdp", "bal"), None),
            P(("fsdp", "bal"), None),
            P(("fsdp", "bal"), None),
            P("fsdp", None),
        ),
        check_vma=False,
    )
```

```python
import functools

import jax
import jax.numpy as jnp
from jax import lax
from jax.experimental import pallas as pl
from jax.experimental.pallas import tpu as pltpu
from jax.sharding import PartitionSpec as P

HEADS = 16
KV_HEADS = 4
HEAD_DIM = 128
REACH = 4

NEG_FILL = -1e30
F32 = jnp.float32
BF16 = jnp.bfloat16


def swap(value, axis, bit):
    count = lax.axis_size(axis)
    return lax.ppermute(value, axis, [(i, i ^ bit) for i in range(count)])


def dot(a, b, ca, cb):
    return lax.dot_general(a, b, (((ca,), (cb,)), ((), ())), preferred_element_type=F32)


def on_chip(shape, dtype=BF16):
    return pltpu.VMEM(shape, dtype)


def run(body, outs, scalars, arrays, scratch=(), room=16, flops=0, exps=0):
    arrays = [pltpu.with_memory_space_constraint(v, pltpu.VMEM) for v in arrays]
    return pl.pallas_call(
        body,
        out_shape=outs,
        in_specs=[pl.BlockSpec(memory_space=pltpu.SMEM)] * len(scalars)
        + [pl.BlockSpec(memory_space=pltpu.VMEM)] * len(arrays),
        out_specs=jax.tree.map(
            lambda _: pl.BlockSpec(memory_space=pltpu.VMEM), outs, is_leaf=lambda v: hasattr(v, "dtype")
        ),
        scratch_shapes=scratch,
        compiler_params=pltpu.CompilerParams(vmem_limit_bytes=room << 20),
        cost_estimate=pl.CostEstimate(flops=flops, transcendentals=exps, bytes_accessed=4 << 20),
        name=getattr(body, "func", body).__name__,
    )(*scalars, *arrays)


def head_of(chip):
    return jnp.bitwise_xor(chip % 2, chip // 2)


def column_of(chip, core):
    return (chip // 2) * (KV_HEADS * HEAD_DIM) + (2 * core + head_of(chip)) * HEAD_DIM


def quarter(z, r, size):
    return pl.ds(pl.multiple_of(jnp.bitwise_xor(z, r) * size, size), size)


def project_rows(z, xs, ws):
    size = ws[0].shape[0]
    total = None
    for r, w in enumerate(ws):
        x = jnp.concatenate([x[:, quarter(z, r, size)] for x in xs], axis=0)
        term = dot(x, w, 1, 0)
        total = term if total is None else total + term
    return total.astype(BF16)


def prep_kernel(ids, block, weight, x, w, x0):
    w[...] = weight[...]
    x0[...] = x[...]


def prepare(ids, block, weight, x):
    size = weight.shape[0]
    whole = pl.BlockSpec(x.shape, lambda i, ids, block: (0, 0))
    return pl.pallas_call(
        prep_kernel,
        out_shape=(on_chip((size, HEAD_DIM)), on_chip(x.shape)),
        grid_spec=pltpu.PrefetchScalarGridSpec(
            num_scalar_prefetch=2,
            grid=(1,),
            in_specs=[pl.BlockSpec((size, HEAD_DIM), lambda i, ids, block: (0, block[0])), whole],
            out_specs=[pl.BlockSpec(memory_space=pltpu.VMEM)] * 2,
        ),
        compiler_params=pltpu.CompilerParams(vmem_limit_bytes=16 << 20),
        name="prep_kernel",
    )(ids, block, *[pltpu.with_memory_space_constraint(v, pltpu.HBM) for v in (weight, x)])


def cut_kernel(x1, x2, top, low):
    half = top.shape[0]
    top[...] = x1[:half, :]
    low[...] = x2[half:, :]


def project_kernel(ids, *refs):
    *xs, w0, w1, w2, w3, out = refs
    out[...] = project_rows(ids[2], xs, (w0[...], w1[...], w2[...], w3[...]))


def window_kernel(ids, *refs):
    *xs, w0, w1, w2, w3, first, o0, o1, o2, o3, kv = refs
    ws = (w0[...], w1[...], w2[...], w3[...])
    m = ids[0]
    rows = first.shape[0] // 3
    for r in range(3):
        kv[r] = first[r * rows : (r + 1) * rows, :]
    kv[3] = project_rows(ids[2], xs, ws)
    for r, out in ((3, o3), (1, o1), (2, o2), (0, o0)):
        target = jnp.bitwise_xor(m, r)
        for w in range(3):
            chip = target + (w - 2)
            rel = jnp.bitwise_xor(jnp.maximum(chip, 0), m)
            out[w * rows : (w + 1) * rows, :] = jnp.where(
                chip >= 0, kv[rel], jnp.zeros((rows, HEAD_DIM), BF16)
            )


def attend_kernel(side, docs, ids, lens, first, second, q_own, q_oth, g_own, g_oth,
                  own, oth, d_first, d_second, bias):
    m, c = ids[0], ids[1]
    rows = q_own.shape[0]
    keys = first.shape[0]
    inv = HEAD_DIM ** (-0.5)
    heads = HEADS // KV_HEADS
    head = head_of(m) if side == 0 else 1 - head_of(m)
    base = (2 * c + head) * (heads * HEAD_DIM)

    def place(chip0, shape, dim):
        t = lax.broadcasted_iota(jnp.int32, shape, dim)
        chip = t // (2 * rows) + chip0
        within = t % (2 * rows)
        mine = within < rows
        shard = 2 * chip + jnp.where(mine, c, 1 - c)
        return shard * rows + jnp.where(mine, within, within - rows)

    kpos = place(m - 2, (keys, 1), 0)
    qpos = place(m, (1, 2 * rows), 1)
    kdoc = jnp.where(kpos >= 0, 0, -1)
    qdoc = jnp.zeros_like(qpos)
    end = jnp.int32(0)
    for k in range(docs):
        end = end + lens[0, k]
        kdoc = kdoc + (kpos >= end).astype(jnp.int32)
        qdoc = qdoc + (qpos >= end).astype(jnp.int32)
    bias[...] = jnp.where((kdoc == qdoc) & (kpos <= qpos), 0.0, NEG_FILL)

    is_key = m < 2
    key = jnp.where(is_key, first[...], second[...])
    val = jnp.where(is_key, second[...], first[...])
    key_t = key.T
    val_t = val.T
    dk = jnp.zeros((keys, HEAD_DIM), F32)
    dv = jnp.zeros((keys, HEAD_DIM), F32)
    for h in range(heads):
        cols = pl.ds(pl.multiple_of(base + h * HEAD_DIM, HEAD_DIM), HEAD_DIM)
        q = jnp.concatenate([q_own[:, cols], q_oth[:, cols]], axis=0)
        g = jnp.concatenate([g_own[:, cols], g_oth[:, cols]], axis=0)
        s = dot(key, q, 1, 1) * inv + bias[...]
        p = jnp.exp(s - jnp.max(s, axis=0, keepdims=True))
        p = p * (1.0 / jnp.sum(p, axis=0, keepdims=True))
        low = p.astype(BF16)
        out_t = dot(val_t, low, 1, 0).astype(BF16).astype(F32)
        delta = jnp.sum(out_t * g.astype(F32).T, axis=0, keepdims=True)
        dp = dot(val, g, 1, 1)
        ds = (p * (dp - delta)).astype(BF16)
        dq_t = dot(key_t, ds, 1, 0) * inv
        dk = dk + dot(ds, q, 1, 0)
        dv = dv + dot(low, g, 1, 0)
        out = out_t.T.astype(BF16)
        dq = dq_t.T.astype(BF16)
        at = slice(h * HEAD_DIM, (h + 1) * HEAD_DIM)
        own[0, :, at] = out[:rows]
        oth[0, :, at] = out[rows:]
        own[1, :, at] = dq[:rows]
        oth[1, :, at] = dq[rows:]
    dk = (dk * inv).astype(BF16)
    dv = dv.astype(BF16)
    d_first[...] = jnp.where(is_key, dk, dv)
    d_second[...] = jnp.where(is_key, dv, dk)


def attend(side, ids, lens, first, second, rest):
    rows = rest[0].shape[0]
    keys = first.shape[0]
    part = on_chip((2, rows, HEADS // KV_HEADS * HEAD_DIM))
    grad = on_chip((keys, HEAD_DIM))
    return run(
        functools.partial(attend_kernel, side, lens.shape[1]),
        (part, part, grad, grad),
        (ids, lens),
        (first, second, *rest),
        scratch=[pltpu.VMEM((keys, 2 * rows), F32)],
        room=24,
        flops=12 * keys * 2 * rows * HEADS // KV_HEADS * HEAD_DIM,
        exps=keys * 2 * rows * HEADS // KV_HEADS,
    )


def place_kernel(ids, own_a, own_b, got_a, got_b, out, dq):
    m, c = ids[0], ids[1]
    width = own_a.shape[2]
    for ref, core, head in (
        (own_a, c, head_of(m)),
        (own_b, c, 1 - head_of(m)),
        (got_a, 1 - c, head_of(m)),
        (got_b, 1 - c, 1 - head_of(m)),
    ):
        cols = pl.ds(pl.multiple_of((2 * core + head) * width, width), width)
        out[:, cols] = ref[0]
        dq[:, cols] = ref[1]


def weight_block(z, r, g_t, xs, size):
    x = jnp.concatenate([x[:, quarter(z, r, size)] for x in xs], axis=0)
    return dot(g_t, x, 1, 0).T


def sum_kernel(ids, *refs):
    d0, d1, d2, d3, *xs, own, oth, g_t, send1, send2, send3, acc = refs
    m, z = ids[0], ids[2]
    rows = own.shape[1]
    acc[...] = jnp.zeros_like(acc)
    for r, d in enumerate((d0, d1, d2, d3)):
        start = pl.multiple_of(jnp.bitwise_xor(m, r) * (2 * rows), 2 * rows)
        span = pl.ds(start, 6 * rows)
        acc[span, :] = acc[span, :] + d[...].astype(F32)
    for r in range(4):
        start = pl.multiple_of((jnp.bitwise_xor(m, r) + 2) * (2 * rows), 2 * rows)
        g = acc[pl.ds(start, 2 * rows), :].astype(BF16)
        own[r] = g[:rows]
        oth[r] = g[rows:]
        g_t[:, r * 2 * rows : (r + 1) * 2 * rows] = g.T
    for r, send in ((3, send3), (2, send2), (1, send1)):
        send[...] = weight_block(z, r, g_t[...], xs, send.shape[0]).astype(BF16)


def keep_kernel(ids, g_t, *refs):
    *xs, keep = refs
    keep[...] = weight_block(ids[2], 0, g_t[...], xs, keep.shape[0])


def fold_kernel(keep, got, now, later):
    now[...] = keep[0] + got[0].astype(F32)
    later[...] = (keep[1] + got[1].astype(F32)).astype(BF16)


def last_kernel(keep, got1, got2, got3, out):
    got = (got1[...].astype(F32) + got2[...].astype(F32)) + got3[...].astype(F32)
    out[...] = (keep[...] + got).astype(BF16)


def assemble_kernel(ids, *refs):
    m, c = ids[0], ids[1]
    out = refs[-1]
    for side in range(2):
        core = c if side == 0 else 1 - c
        for r in range(4):
            col = pl.multiple_of(column_of(jnp.bitwise_xor(m, r), core), HEAD_DIM)
            out[:, pl.ds(col, HEAD_DIM)] = refs[4 * side + r][...].astype(F32)


def token_kernel(own, oth, w0, w1, w2, w3, u0, u1, u2, u3, send_a, send_b, keep_a, keep_b):
    rows = own.shape[1]
    g = jnp.concatenate(
        [jnp.concatenate([own[r] for r in range(4)], axis=0),
         jnp.concatenate([oth[r] for r in range(4)], axis=0)], axis=1)
    ws = (w0[...], w1[...], w2[...], w3[...])
    us = (u0[...], u1[...], u2[...], u3[...])
    size = w0.shape[0]
    for i in range(4):
        w = jnp.concatenate([ws[i], us[i]], axis=1)
        t = dot(g, w, 1, 1)
        at = slice((i % 2) * size, (i % 2 + 1) * size)
        send, keep, away = (send_a, keep_a, (1, 3)) if i < 2 else (send_b, keep_b, (2, 3))
        home = [r for r in range(4) if r not in away]
        for k in range(2):
            send[k, :, at] = t[away[k] * rows : (away[k] + 1) * rows].astype(BF16)
            keep[k, :, at] = t[home[k] * rows : (home[k] + 1) * rows]


def fold_both_kernel(keep_a, got_a, keep_b, got_b, a, a_send, b, b_send):
    fold_kernel(keep_a, got_a, a, a_send)
    fold_kernel(keep_b, got_b, b, b_send)


def token_last_kernel(ids, a, got_a, b, got_b, out):
    size = out.shape[1] // 4
    for i in range(4):
        now, got = (a, got_a) if i < 2 else (b, got_b)
        at = slice((i % 2) * size, (i % 2 + 1) * size)
        out[:, quarter(ids[2], i, size)] = (now[:, at] + got[:, at].astype(F32)).astype(BF16)


def plane_local(tokens, kv_weight, queries, out_grad, doc_lengths):
    rows, width = tokens.shape
    size = kv_weight.shape[0]
    m, c = lax.axis_index("bal") // 2, lax.axis_index("bal") % 2
    ids = jnp.stack([m, c, lax.axis_index("fsdp")]).astype(jnp.int32)
    pair = lambda v: swap(v, "bal", 1)
    near = lambda v: swap(v, "bal", 2)
    far = lambda v: swap(v, "bal", 4)
    cross = lambda v: swap(v, "bal", 6)

    x1, x2 = near(tokens), far(tokens)
    block = (column_of(m, c) // HEAD_DIM).astype(jnp.int32).reshape(1)
    w0, x0 = prepare(ids, block, kv_weight, tokens)
    w2, w1 = swap(w0, "fsdp", 2), swap(w0, "fsdp", 1)
    x1, x2, w1, w2 = lax.optimization_barrier((x1, x2, w1, w2))
    w3 = swap(w2, "fsdp", 1)
    ws = (w0, w1, w2, w3)
    half = on_chip((rows // 2, width))
    top, low = run(cut_kernel, (half, half), (), (x1, x2))
    x3 = [far(top), near(low)]
    flip = lambda vs: [pair(v) for v in vs]
    early = (x0, pair(x0), x1, pair(x1), x2, pair(x2))
    first = run(project_kernel, on_chip((6 * rows, HEAD_DIM)), (ids,), early + ws)
    *x3, first = lax.optimization_barrier((*x3, first))
    late = (*x3, *flip(x3))
    xs = early + late

    rest = (queries, pair(queries), out_grad, pair(out_grad))
    us = tuple(flip(ws))

    win = run(
        window_kernel,
        (on_chip((6 * rows, HEAD_DIM)),) * 4,
        (ids,),
        late + ws + (first,),
        scratch=[pltpu.VMEM((4, 2 * rows, HEAD_DIM), BF16)],
    )
    win3, win1, win2 = lax.optimization_barrier((cross(win[3]), win[1], win[2]))
    win1, win2 = near(win1), far(win2)

    own_a, oth_a, d0, d3 = attend(0, ids, doc_lengths, win[0], win3, rest)
    d3 = cross(d3)
    got_a = pair(oth_a)
    win1, win2, d0 = lax.optimization_barrier((win1, win2, d0))
    own_b, oth_b, d1, d2 = attend(1, ids, doc_lengths, win1, win2, rest)
    d1, d2, d3, got_a, us = lax.optimization_barrier((d1, d2, d3, got_a, us))
    d1, d2 = near(d1), far(d2)
    got_b = pair(oth_b)
    like = jax.ShapeDtypeStruct(queries.shape, BF16)
    attn_out, grad_queries = run(place_kernel, (like, like), (ids,), (own_a, own_b, got_a, got_b))

    block = on_chip((4, rows, HEAD_DIM))
    third = on_chip((size, HEAD_DIM))
    g_own, g_oth, g_t, *sends = run(
        sum_kernel,
        (block, block, on_chip((HEAD_DIM, 8 * rows)), third, third, third),
        (ids,),
        (d0, d1, d2, d3) + xs,
        scratch=[pltpu.VMEM((12 * rows, HEAD_DIM), F32)],
    )
    gots = [swap(v, "fsdp", bit) for v, bit in zip(sends, (1, 2, 3))]
    g_oth = pair(g_oth)
    g_t, g_oth = lax.optimization_barrier((g_t, g_oth))
    half = (rows, width // 2)
    send_a, send_b, keep_a, keep_b = run(
        token_kernel,
        (on_chip((2, *half)), on_chip((2, *half)), on_chip((2, *half), F32), on_chip((2, *half), F32)),
        (),
        (g_own, g_oth) + ws + us,
    )
    got_a, got_b = near(send_a), far(send_b)
    keep = run(keep_kernel, on_chip((size, HEAD_DIM), F32), (ids,), (g_t,) + xs)
    *gots, attn_out, grad_queries = lax.optimization_barrier((*gots, attn_out, grad_queries))
    mine = run(last_kernel, on_chip((size, HEAD_DIM)), (), (keep, *gots))
    fold = (on_chip(half, F32), on_chip(half))
    a, a_send, b, b_send = run(fold_both_kernel, fold + fold, (), (keep_a, got_a, keep_b, got_b))
    got_a, got_b = far(a_send), near(b_send)
    mine = [mine, near(mine), far(mine), cross(mine)]
    theirs = [pair(v) for v in mine]
    grad_weight = run(
        assemble_kernel,
        jax.ShapeDtypeStruct((size, kv_weight.shape[1]), F32),
        (ids,),
        mine + theirs,
    )
    grad_tokens = run(
        token_last_kernel, jax.ShapeDtypeStruct(tokens.shape, BF16), (ids,), (a, got_a, b, got_b)
    )
    return attn_out, grad_queries, grad_tokens, grad_weight


def from_behind(value, axis, steps):
    count = lax.axis_size(axis)
    initial, last = (max(0, -steps), min(count, count - steps))
    return lax.ppermute(value, axis, [(source, source + steps) for source in range(initial, last)])


def doc_index(doc_ends, positions):
    return jnp.sum((doc_ends[None, :] <= positions[:, None]).astype(jnp.int32), axis=1)


def score_tile(q_group, key_block, mask_block, inv_root):
    raw_scores = (
        jnp.einsum("qhd,kd->hqk", q_group, key_block, preferred_element_type=jnp.float32) * inv_root
    )
    return jnp.where(mask_block[None], raw_scores, NEG_FILL)


def value_tile(prob_tile, value_block):
    return jnp.einsum("hqk,kd->qhd", prob_tile, value_block, preferred_element_type=jnp.float32)


def dprob_tile(grad_group, value_block):
    return jnp.einsum("qhd,kd->hqk", grad_group, value_block, preferred_element_type=jnp.float32)


def query_tile(dscore_tile, key_block):
    return jnp.einsum("hqk,kd->qhd", dscore_tile, key_block, preferred_element_type=jnp.float32)


def key_tile(dscore_tile, q_group, inv_root):
    return (
        jnp.einsum("hqk,qhd->kd", dscore_tile, q_group, preferred_element_type=jnp.float32)
        * inv_root
    )


def value_grad_tile(prob_tile, grad_group):
    return jnp.einsum("hqk,qhd->kd", prob_tile, grad_group, preferred_element_type=jnp.float32)


def attend_rows(q_rows, kv_blocks, grad_rows, allowed_parts):
    row_count = q_rows.shape[0]
    key_rows = kv_blocks[0].shape[0]
    group_size = HEADS // KV_HEADS
    inv_root = HEAD_DIM ** (-0.5)
    window_range = list(range(len(kv_blocks)))
    row_shape = (row_count, group_size, HEAD_DIM)
    out_parts = []
    dq_parts = []
    key_grads = [[] for window_pos in window_range]
    value_grads = [[] for window_pos in window_range]
    for head_group in range(KV_HEADS):
        col_start = head_group * group_size * HEAD_DIM
        col_stop = col_start + group_size * HEAD_DIM
        val_start = (KV_HEADS + head_group) * HEAD_DIM
        q_group = q_rows[:, col_start:col_stop].reshape(row_shape)
        grad_group = grad_rows[:, col_start:col_stop].reshape(row_shape)
        key_list = [
            piece[:, head_group * HEAD_DIM : (head_group + 1) * HEAD_DIM] for piece in kv_blocks
        ]
        value_list = [piece[:, val_start : val_start + HEAD_DIM] for piece in kv_blocks]
        score_tiles = [
            score_tile(q_group, key_list[window_pos], allowed_parts[window_pos], inv_root)
            for window_pos in window_range
        ]
        scores = jnp.concatenate(score_tiles, axis=2)
        row_max = jnp.max(scores, axis=-1, keepdims=True)
        exp_shift = jnp.exp(scores - row_max)
        prob_full = exp_shift / jnp.sum(exp_shift, axis=-1, keepdims=True)
        prob_low = prob_full.astype(jnp.bfloat16)
        prob_tiles = [
            prob_low[:, :, window_pos * key_rows : (window_pos + 1) * key_rows]
            for window_pos in window_range
        ]
        out_accum = jnp.zeros(row_shape, jnp.float32)
        for window_pos in window_range:
            out_accum = out_accum + value_tile(prob_tiles[window_pos], value_list[window_pos])
        out_group = out_accum.astype(jnp.bfloat16)
        row_delta = jnp.sum(grad_group.astype(jnp.float32) * out_group.astype(jnp.float32), axis=-1)
        dprob_tiles = [
            dprob_tile(grad_group, value_list[window_pos]) for window_pos in window_range
        ]
        dprobs = jnp.concatenate(dprob_tiles, axis=2)
        dscores = (prob_full * (dprobs - row_delta.T[:, :, None])).astype(jnp.bfloat16)
        dq_accum = jnp.zeros(row_shape, jnp.float32)
        for window_pos in window_range:
            dscore_piece = dscores[:, :, window_pos * key_rows : (window_pos + 1) * key_rows]
            dq_accum = dq_accum + query_tile(dscore_piece, key_list[window_pos])
            key_grads[window_pos].append(key_tile(dscore_piece, q_group, inv_root))
            value_grads[window_pos].append(value_grad_tile(prob_tiles[window_pos], grad_group))
        dq_group = (dq_accum * inv_root).astype(jnp.bfloat16)
        out_parts.append(out_group.reshape(row_count, group_size * HEAD_DIM))
        dq_parts.append(dq_group.reshape(row_count, group_size * HEAD_DIM))
    window_terms = [
        jnp.concatenate(key_grads[window_pos] + value_grads[window_pos], axis=1)
        for window_pos in window_range
    ]
    return (jnp.concatenate(out_parts, axis=1), jnp.concatenate(dq_parts, axis=1), window_terms)


def local(tokens, kv_weight, queries, out_grad, doc_lengths):
    row_count = tokens.shape[0]
    bal_index = lax.axis_index("bal")
    doc_ends = jnp.cumsum(doc_lengths[0])
    row_ids = jnp.arange(row_count, dtype=jnp.int32)
    own_pos = bal_index * row_count + row_ids
    own_doc = doc_index(doc_ends, own_pos)
    allowed_parts = []
    for distance in range(REACH, -1, -1):
        key_pos = (bal_index - distance) * row_count + row_ids
        key_doc = jnp.where(key_pos >= 0, doc_index(doc_ends, key_pos), -1)
        allowed_parts.append(
            (own_doc[:, None] == key_doc[None, :]) & (key_pos[None, :] <= own_pos[:, None])
        )
    full_weight = lax.all_gather(kv_weight, "fsdp", axis=0, tiled=True)
    kv_accum = jnp.dot(tokens, full_weight, preferred_element_type=jnp.float32)
    kv_rows = kv_accum.astype(jnp.bfloat16)
    earlier = [kv_rows]
    for distance in range(1, REACH + 1):
        earlier.append(from_behind(kv_rows, "bal", distance))
    kv_blocks = earlier[::-1]
    attn_out, grad_queries, window_terms = attend_rows(queries, kv_blocks, out_grad, allowed_parts)
    grad_terms = window_terms[::-1]
    grad_sum = grad_terms[0]
    for distance in range(1, REACH + 1):
        grad_sum = grad_sum + from_behind(
            grad_terms[distance].astype(jnp.bfloat16), "bal", -distance
        ).astype(jnp.float32)
    grad_kv = grad_sum.astype(jnp.bfloat16)
    grad_tokens = lax.dot_general(
        grad_kv, full_weight, (((1,), (1,)), ((), ())), preferred_element_type=jnp.float32
    ).astype(jnp.bfloat16)
    shard_sum = lax.psum_scatter(
        lax.dot_general(
            tokens, grad_kv, (((0,), (0,)), ((), ())), preferred_element_type=jnp.float32
        ).astype(jnp.bfloat16),
        "fsdp",
        scatter_dimension=0,
        tiled=True,
    )
    grad_weight = lax.psum(shard_sum, "bal").astype(jnp.float32)
    return (attn_out, grad_queries, grad_tokens, grad_weight)


def solution(mesh):
    placed = (
        P(("fsdp", "bal"), None),
        P("fsdp", None),
        P(("fsdp", "bal"), None),
        P(("fsdp", "bal"), None),
        P("fsdp", None),
    )
    one_plane = mesh.shape["bal"] == 8 and mesh.shape["fsdp"] == 4
    return jax.shard_map(
        plane_local if one_plane else local,
        mesh=mesh,
        in_specs=placed,
        out_specs=(
            P(("fsdp", "bal"), None),
            P(("fsdp", "bal"), None),
            P(("fsdp", "bal"), None),
            P("fsdp", None),
        ),
        check_vma=False,
    )
```

```python
import functools

import jax
import jax.numpy as jnp
from jax import lax
from jax.experimental import pallas as pl
from jax.experimental.pallas import tpu as pltpu
from jax.sharding import PartitionSpec as P

HEADS = 16
KV_HEADS = 4
HEAD_DIM = 128
REACH = 4

NEG_FILL = -1e30
F32 = jnp.float32
BF16 = jnp.bfloat16


def swap(value, axis, bit):
    count = lax.axis_size(axis)
    return lax.ppermute(value, axis, [(i, i ^ bit) for i in range(count)])


def dot(a, b, ca, cb):
    return lax.dot_general(a, b, (((ca,), (cb,)), ((), ())), preferred_element_type=F32)


def on_chip(shape, dtype=BF16):
    return pltpu.VMEM(shape, dtype)


def run(body, outs, scalars, arrays, scratch=(), room=16):
    arrays = [pltpu.with_memory_space_constraint(v, pltpu.VMEM) for v in arrays]
    return pl.pallas_call(
        body,
        out_shape=outs,
        in_specs=[pl.BlockSpec(memory_space=pltpu.SMEM)] * len(scalars)
        + [pl.BlockSpec(memory_space=pltpu.VMEM)] * len(arrays),
        out_specs=jax.tree.map(
            lambda _: pl.BlockSpec(memory_space=pltpu.VMEM), outs, is_leaf=lambda v: hasattr(v, "dtype")
        ),
        scratch_shapes=scratch,
        compiler_params=pltpu.CompilerParams(vmem_limit_bytes=room << 20),
        name=getattr(body, "func", body).__name__,
    )(*scalars, *arrays)


def column_of(chip, core):
    return core * (KV_HEADS * HEAD_DIM) + chip * HEAD_DIM


def quarter(z, r, size):
    return pl.ds(pl.multiple_of(jnp.bitwise_xor(z, r) * size, size), size)


def project_rows(z, xs, ws):
    size = ws[0].shape[0]
    total = None
    for r, w in enumerate(ws):
        x = jnp.concatenate([x[:, quarter(z, r, size)] for x in xs], axis=0)
        term = dot(x, w, 1, 0)
        total = term if total is None else total + term
    return total.astype(BF16)


def prep_kernel(ids, block, weight, x, w, x0):
    w[...] = weight[...]
    x0[...] = x[...]


def prepare(ids, block, weight, x):
    size = weight.shape[0]
    whole = pl.BlockSpec(x.shape, lambda i, ids, block: (0, 0))
    return pl.pallas_call(
        prep_kernel,
        out_shape=(on_chip((size, HEAD_DIM)), on_chip(x.shape)),
        grid_spec=pltpu.PrefetchScalarGridSpec(
            num_scalar_prefetch=2,
            grid=(1,),
            in_specs=[pl.BlockSpec((size, HEAD_DIM), lambda i, ids, block: (0, block[0])), whole],
            out_specs=[pl.BlockSpec(memory_space=pltpu.VMEM)] * 2,
        ),
        compiler_params=pltpu.CompilerParams(vmem_limit_bytes=16 << 20),
        name="prep_kernel",
    )(ids, block, *[pltpu.with_memory_space_constraint(v, pltpu.HBM) for v in (weight, x)])


def cut_kernel(x1, x2, top, low):
    half = top.shape[0]
    top[...] = x1[:half, :]
    low[...] = x2[half:, :]


def project_kernel(ids, *refs):
    *xs, w0, w1, w2, w3, out = refs
    out[...] = project_rows(ids[2], xs, (w0[...], w1[...], w2[...], w3[...]))


def order_kernel(ids, *refs):
    *xs, w0, w1, w2, w3, first, out = refs
    m, c, z = ids[0], ids[1], ids[2]
    chip_rows = first.shape[0] // 3
    rows = chip_rows // 2
    last = project_rows(z, xs, (w0[...], w1[...], w2[...], w3[...]))
    for r in range(4):
        part = first[r * chip_rows : (r + 1) * chip_rows, :] if r < 3 else last
        chip = jnp.bitwise_xor(m, r)
        out[shard_rows(2 * chip + c, rows), :] = part[:rows]
        out[shard_rows(2 * chip + 1 - c, rows), :] = part[rows:]


def shard_rows(shard, rows, count=1):
    return pl.ds(pl.multiple_of(shard * rows, rows), rows * count)


def cut_heads_kernel(ids, *refs):
    for r in range(4):
        refs[8 + r][0] = refs[2 * r][...]
        refs[8 + r][1] = refs[2 * r + 1][...]


def cut_heads(ids, queries, out_grad):
    rows = queries.shape[0]
    width = queries.shape[1] // KV_HEADS
    both = [pltpu.with_memory_space_constraint(v, pltpu.HBM) for v in (queries, out_grad)]
    return pl.pallas_call(
        cut_heads_kernel,
        out_shape=(on_chip((2, rows, width)),) * 4,
        grid_spec=pltpu.PrefetchScalarGridSpec(
            num_scalar_prefetch=1,
            grid=(1,),
            in_specs=[
                pl.BlockSpec((rows, width), lambda i, ids, r=r: (0, jnp.bitwise_xor(ids[0], r)))
                for r in (0, 0, 1, 1, 2, 2, 3, 3)
            ],
            out_specs=[pl.BlockSpec(memory_space=pltpu.VMEM)] * 4,
        ),
        compiler_params=pltpu.CompilerParams(vmem_limit_bytes=16 << 20),
        name="cut_heads_kernel",
    )(ids, *(both * 4))


def attend_kernel(rels, docs, first_call, last_call, ids, lens, mine, got, *refs):
    count = len(rels)
    qgs, refs = refs[:count], refs[count:]
    if not first_call:
        dk_in, dv_in = refs[:2]
        refs = refs[2:]
    outs, refs = refs[:count], refs[count:]
    if last_call:
        own, send, *refs = refs
    dk, dv, key, val, key_t, val_t = refs
    m, c = ids[0], ids[1]
    rows = qgs[0].shape[1]
    keys = mine.shape[0]
    heads = HEADS // KV_HEADS
    inv = HEAD_DIM ** (-0.5)
    is_key = c == 0
    key[...] = jnp.where(is_key, mine[...], got[...])
    val[...] = jnp.where(is_key, got[...], mine[...])
    key_t[...] = key[...].T
    val_t[...] = val[...].T
    if first_call:
        dk[...] = jnp.zeros_like(dk)
        dv[...] = jnp.zeros_like(dv)
    else:
        dk[...] = dk_in[...]
        dv[...] = dv_in[...]

    def body(i, shard, begin, shards):
        span = shard_rows(begin, rows, shards)
        size = shards * rows
        kpos = lax.broadcasted_iota(jnp.int32, (size, 1), 0) + begin * rows
        qpos = lax.broadcasted_iota(jnp.int32, (1, rows), 1) + shard * rows
        kdoc = jnp.zeros_like(kpos)
        qdoc = jnp.zeros_like(qpos)
        end = jnp.int32(0)
        for k in range(docs):
            end = end + lens[0, k]
            kdoc = kdoc + (kpos >= end).astype(jnp.int32)
            qdoc = qdoc + (qpos >= end).astype(jnp.int32)
        bias = jnp.where((kdoc == qdoc) & (kpos <= qpos), 0.0, NEG_FILL)
        bias = jnp.concatenate([bias, bias], axis=1)
        k, v, k_t, v_t = key[span, :], val[span, :], key_t[:, span], val_t[:, span]
        grads_k, grads_v = [], []
        for h in range(0, heads, 2):
            cols = [slice((h + e) * HEAD_DIM, (h + e + 1) * HEAD_DIM) for e in range(2)]
            q = jnp.concatenate([qgs[i][0, :, at] for at in cols], axis=0)
            g = jnp.concatenate([qgs[i][1, :, at] for at in cols], axis=0)
            s = dot(k, q, 1, 1) * inv + bias
            p = jnp.exp(s - jnp.max(s, axis=0, keepdims=True))
            p = p * (1.0 / jnp.sum(p, axis=0, keepdims=True))
            low = p.astype(BF16)
            out_t = dot(v_t, low, 1, 0).astype(BF16).astype(F32)
            delta = jnp.sum(out_t * g.astype(F32).T, axis=0, keepdims=True)
            ds = (p * (dot(v, g, 1, 1) - delta)).astype(BF16)
            dq_t = dot(k_t, ds, 1, 0) * inv
            grads_k.append(dot(ds, q, 1, 0))
            grads_v.append(dot(low, g, 1, 0))
            out = out_t.T.astype(BF16)
            dq = dq_t.T.astype(BF16)
            for e, at in enumerate(cols):
                outs[i][0, :, at] = out[e * rows : (e + 1) * rows]
                outs[i][1, :, at] = dq[e * rows : (e + 1) * rows]
        dk[span, :] = dk[span, :] + (grads_k[0] + grads_k[1]) * inv
        dv[span, :] = dv[span, :] + (grads_v[0] + grads_v[1])

    for i, r in enumerate(rels):
        chip = jnp.bitwise_xor(m, r)
        shard = 2 * chip + c

        @pl.when(chip == 0)
        def _():
            body(i, shard, 0, 2)

        @pl.when(chip > 0)
        def _():
            body(i, shard, jnp.maximum(shard - REACH, 0), REACH + 1)

    if last_call:
        own[...] = jnp.where(is_key, dk[...], dv[...])
        send[...] = jnp.where(is_key, dv[...], dk[...]).astype(BF16)


def attend(rels, ids, lens, mine, got, qgs, sums=(), last=False):
    keys = mine.shape[0]
    total = (keys, HEAD_DIM)
    wide, tall = pltpu.VMEM(total, BF16), pltpu.VMEM((HEAD_DIM, keys), BF16)
    sides = (on_chip(total, F32), on_chip(total) if last else on_chip(total, F32))
    *outs, first, second = run(
        functools.partial(attend_kernel, rels, lens.shape[1], not sums, last),
        tuple(on_chip(v.shape) for v in qgs) + sides,
        (ids, lens),
        (mine, got, *qgs, *sums),
        scratch=([pltpu.VMEM(total, F32)] * 2 if last else []) + [wide, wide, tall, tall],
        room=24,
    )
    return outs, (first, second)


def place_kernel(ids, p0, p1, p2, p3, out, dq):
    width = p0.shape[2]
    for r, part in enumerate((p0, p1, p2, p3)):
        cols = quarter(ids[0], r, width)
        out[:, cols] = part[0]
        dq[:, cols] = part[1]


def weight_block(z, r, g_t, xs, size):
    x = jnp.concatenate([x[:, quarter(z, r, size)] for x in xs], axis=0)
    return dot(g_t, x, 1, 0).T


def sum_kernel(ids, mine, got, own, oth):
    m, c = ids[0], ids[1]
    rows = own.shape[1]
    for r in range(4):
        chip = jnp.bitwise_xor(m, r)
        for core, out in ((c, own), (1 - c, oth)):
            span = shard_rows(2 * chip + core, rows)
            out[r] = (mine[span, :] + got[span, :].astype(F32)).astype(BF16)


def weight_kernel(ids, own, oth, *refs):
    *xs, keep, send1, send2, send3, g_t = refs
    z = ids[2]
    rows = own.shape[1]
    for r in range(4):
        g_t[:, 2 * r * rows : (2 * r + 1) * rows] = own[r].T
        g_t[:, (2 * r + 1) * rows : (2 * r + 2) * rows] = oth[r].T
    for r, send in ((3, send3), (2, send2), (1, send1)):
        send[...] = weight_block(z, r, g_t[...], xs, send.shape[0]).astype(BF16)
    keep[...] = weight_block(z, 0, g_t[...], xs, keep.shape[0])


def fold_kernel(keep, got, now, later):
    now[...] = keep[0] + got[0].astype(F32)
    later[...] = (keep[1] + got[1].astype(F32)).astype(BF16)


def last_kernel(keep, got1, got2, got3, out):
    got = (got1[...].astype(F32) + got2[...].astype(F32)) + got3[...].astype(F32)
    out[...] = (keep[...] + got).astype(BF16)


def assemble_kernel(ids, *refs):
    m, c = ids[0], ids[1]
    out = refs[-1]
    for side in range(2):
        core = c if side == 0 else 1 - c
        for r in range(4):
            col = pl.multiple_of(column_of(jnp.bitwise_xor(m, r), core), HEAD_DIM)
            out[:, pl.ds(col, HEAD_DIM)] = refs[4 * side + r][...].astype(F32)


def token_kernel(own, oth, w0, w1, w2, w3, u0, u1, u2, u3, send_a, send_b, keep_a, keep_b):
    rows = own.shape[1]
    g = jnp.concatenate(
        [jnp.concatenate([own[r] for r in range(4)], axis=0),
         jnp.concatenate([oth[r] for r in range(4)], axis=0)], axis=1)
    ws = (w0[...], w1[...], w2[...], w3[...])
    us = (u0[...], u1[...], u2[...], u3[...])
    size = w0.shape[0]
    for i in range(4):
        w = jnp.concatenate([ws[i], us[i]], axis=1)
        t = dot(g, w, 1, 1)
        at = slice((i % 2) * size, (i % 2 + 1) * size)
        send, keep, away = (send_a, keep_a, (1, 3)) if i < 2 else (send_b, keep_b, (2, 3))
        home = [r for r in range(4) if r not in away]
        for k in range(2):
            send[k, :, at] = t[away[k] * rows : (away[k] + 1) * rows].astype(BF16)
            keep[k, :, at] = t[home[k] * rows : (home[k] + 1) * rows]


def fold_both_kernel(keep_a, got_a, keep_b, got_b, a, a_send, b, b_send):
    fold_kernel(keep_a, got_a, a, a_send)
    fold_kernel(keep_b, got_b, b, b_send)


def token_last_kernel(ids, a, got_a, b, got_b, out):
    size = out.shape[1] // 4
    for i in range(4):
        now, got = (a, got_a) if i < 2 else (b, got_b)
        at = slice((i % 2) * size, (i % 2 + 1) * size)
        out[:, quarter(ids[2], i, size)] = (now[:, at] + got[:, at].astype(F32)).astype(BF16)


def plane_local(tokens, kv_weight, queries, out_grad, doc_lengths):
    rows, width = tokens.shape
    size = kv_weight.shape[0]
    m, c = lax.axis_index("bal") // 2, lax.axis_index("bal") % 2
    ids = jnp.stack([m, c, lax.axis_index("fsdp")]).astype(jnp.int32)
    pair = lambda v: swap(v, "bal", 1)
    near = lambda v: swap(v, "bal", 2)
    far = lambda v: swap(v, "bal", 4)
    cross = lambda v: swap(v, "bal", 6)

    x1, x2 = near(tokens), far(tokens)
    block = (column_of(m, c) // HEAD_DIM).astype(jnp.int32).reshape(1)
    w0, x0 = prepare(ids, block, kv_weight, tokens)
    w2, w1 = swap(w0, "fsdp", 2), swap(w0, "fsdp", 1)
    x1, x2, w1, w2 = lax.optimization_barrier((x1, x2, w1, w2))
    w3 = swap(w2, "fsdp", 1)
    ws = (w0, w1, w2, w3)
    half = on_chip((rows // 2, width))
    top, low = run(cut_kernel, (half, half), (), (x1, x2))
    x3 = [far(top), near(low)]
    flip = lambda vs: [pair(v) for v in vs]
    early = (x0, pair(x0), x1, pair(x1), x2, pair(x2))
    first = run(project_kernel, on_chip((6 * rows, HEAD_DIM)), (ids,), early + ws)
    *x3, first = lax.optimization_barrier((*x3, first))
    us = tuple(flip(ws))
    p0, *away = cut_heads(ids, queries, out_grad)
    p1, p2, p3 = away
    p1, p2 = near(p1), far(p2)
    late = (*x3, *flip(x3))
    xs = early + late
    p1, p2, p3, first = lax.optimization_barrier((p1, p2, p3, first))
    mine = run(order_kernel, on_chip((8 * rows, HEAD_DIM)), (ids,), late + ws + (first,))
    p3 = cross(p3)
    got = pair(mine)
    (o0,), sums = attend((0,), ids, doc_lengths, mine, got, (p0,))
    p1, p2, *sums = lax.optimization_barrier((p1, p2, *sums))
    (o1, o2), sums = attend((1, 2), ids, doc_lengths, mine, got, (p1, p2), sums)
    o1, o2 = near(o1), far(o2)
    p3, *sums = lax.optimization_barrier((p3, *sums))
    (o3,), (g_mine, g_send) = attend((3,), ids, doc_lengths, mine, got, (p3,), sums, True)
    g_send, us = lax.optimization_barrier((g_send, us))
    g_got = pair(g_send)
    o3 = cross(o3)

    block = on_chip((4, rows, HEAD_DIM))
    third = on_chip((size, HEAD_DIM))
    g_own, g_oth = run(sum_kernel, (block, block), (ids,), (g_mine, g_got))
    g_got = pair(g_oth)
    half = (rows, width // 2)
    send_a, send_b, keep_a, keep_b = run(
        token_kernel,
        (on_chip((2, *half)), on_chip((2, *half)), on_chip((2, *half), F32), on_chip((2, *half), F32)),
        (),
        (g_own, g_got) + ws + us,
    )
    got_a, got_b = near(send_a), far(send_b)
    keep, *sends = run(
        weight_kernel,
        (on_chip((size, HEAD_DIM), F32), third, third, third),
        (ids,),
        (g_own, g_oth) + xs,
        scratch=[pltpu.VMEM((HEAD_DIM, 8 * rows), BF16)],
    )
    gots = [swap(v, "fsdp", bit) for v, bit in zip(sends, (1, 2, 3))]
    mine = run(last_kernel, on_chip((size, HEAD_DIM)), (), (keep, *gots))
    got_a, got_b, mine = lax.optimization_barrier((got_a, got_b, mine))
    fold = (on_chip(half, F32), on_chip(half))
    a, a_send, b, b_send = run(fold_both_kernel, fold + fold, (), (keep_a, got_a, keep_b, got_b))
    got_a, got_b = far(a_send), near(b_send)
    like = jax.ShapeDtypeStruct(queries.shape, BF16)
    attn_out, grad_queries = run(place_kernel, (like, like), (ids,), (o0, o1, o2, o3))
    mine = [mine, near(mine), far(mine), cross(mine)]
    *mine, attn_out, grad_queries = lax.optimization_barrier((*mine, attn_out, grad_queries))
    theirs = [pair(v) for v in mine]
    grad_weight = run(
        assemble_kernel,
        jax.ShapeDtypeStruct((size, kv_weight.shape[1]), F32),
        (ids,),
        mine + theirs,
    )
    grad_tokens = run(
        token_last_kernel, jax.ShapeDtypeStruct(tokens.shape, BF16), (ids,), (a, got_a, b, got_b)
    )
    return attn_out, grad_queries, grad_tokens, grad_weight


def from_behind(value, axis, steps):
    count = lax.axis_size(axis)
    initial, last = (max(0, -steps), min(count, count - steps))
    return lax.ppermute(value, axis, [(source, source + steps) for source in range(initial, last)])


def doc_index(doc_ends, positions):
    return jnp.sum((doc_ends[None, :] <= positions[:, None]).astype(jnp.int32), axis=1)


def score_tile(q_group, key_block, mask_block, inv_root):
    raw_scores = (
        jnp.einsum("qhd,kd->hqk", q_group, key_block, preferred_element_type=jnp.float32) * inv_root
    )
    return jnp.where(mask_block[None], raw_scores, NEG_FILL)


def value_tile(prob_tile, value_block):
    return jnp.einsum("hqk,kd->qhd", prob_tile, value_block, preferred_element_type=jnp.float32)


def dprob_tile(grad_group, value_block):
    return jnp.einsum("qhd,kd->hqk", grad_group, value_block, preferred_element_type=jnp.float32)


def query_tile(dscore_tile, key_block):
    return jnp.einsum("hqk,kd->qhd", dscore_tile, key_block, preferred_element_type=jnp.float32)


def key_tile(dscore_tile, q_group, inv_root):
    return (
        jnp.einsum("hqk,qhd->kd", dscore_tile, q_group, preferred_element_type=jnp.float32)
        * inv_root
    )


def value_grad_tile(prob_tile, grad_group):
    return jnp.einsum("hqk,qhd->kd", prob_tile, grad_group, preferred_element_type=jnp.float32)


def attend_rows(q_rows, kv_blocks, grad_rows, allowed_parts):
    row_count = q_rows.shape[0]
    key_rows = kv_blocks[0].shape[0]
    group_size = HEADS // KV_HEADS
    inv_root = HEAD_DIM ** (-0.5)
    window_range = list(range(len(kv_blocks)))
    row_shape = (row_count, group_size, HEAD_DIM)
    out_parts = []
    dq_parts = []
    key_grads = [[] for window_pos in window_range]
    value_grads = [[] for window_pos in window_range]
    for head_group in range(KV_HEADS):
        col_start = head_group * group_size * HEAD_DIM
        col_stop = col_start + group_size * HEAD_DIM
        val_start = (KV_HEADS + head_group) * HEAD_DIM
        q_group = q_rows[:, col_start:col_stop].reshape(row_shape)
        grad_group = grad_rows[:, col_start:col_stop].reshape(row_shape)
        key_list = [
            piece[:, head_group * HEAD_DIM : (head_group + 1) * HEAD_DIM] for piece in kv_blocks
        ]
        value_list = [piece[:, val_start : val_start + HEAD_DIM] for piece in kv_blocks]
        score_tiles = [
            score_tile(q_group, key_list[window_pos], allowed_parts[window_pos], inv_root)
            for window_pos in window_range
        ]
        scores = jnp.concatenate(score_tiles, axis=2)
        row_max = jnp.max(scores, axis=-1, keepdims=True)
        exp_shift = jnp.exp(scores - row_max)
        prob_full = exp_shift / jnp.sum(exp_shift, axis=-1, keepdims=True)
        prob_low = prob_full.astype(jnp.bfloat16)
        prob_tiles = [
            prob_low[:, :, window_pos * key_rows : (window_pos + 1) * key_rows]
            for window_pos in window_range
        ]
        out_accum = jnp.zeros(row_shape, jnp.float32)
        for window_pos in window_range:
            out_accum = out_accum + value_tile(prob_tiles[window_pos], value_list[window_pos])
        out_group = out_accum.astype(jnp.bfloat16)
        row_delta = jnp.sum(grad_group.astype(jnp.float32) * out_group.astype(jnp.float32), axis=-1)
        dprob_tiles = [
            dprob_tile(grad_group, value_list[window_pos]) for window_pos in window_range
        ]
        dprobs = jnp.concatenate(dprob_tiles, axis=2)
        dscores = (prob_full * (dprobs - row_delta.T[:, :, None])).astype(jnp.bfloat16)
        dq_accum = jnp.zeros(row_shape, jnp.float32)
        for window_pos in window_range:
            dscore_piece = dscores[:, :, window_pos * key_rows : (window_pos + 1) * key_rows]
            dq_accum = dq_accum + query_tile(dscore_piece, key_list[window_pos])
            key_grads[window_pos].append(key_tile(dscore_piece, q_group, inv_root))
            value_grads[window_pos].append(value_grad_tile(prob_tiles[window_pos], grad_group))
        dq_group = (dq_accum * inv_root).astype(jnp.bfloat16)
        out_parts.append(out_group.reshape(row_count, group_size * HEAD_DIM))
        dq_parts.append(dq_group.reshape(row_count, group_size * HEAD_DIM))
    window_terms = [
        jnp.concatenate(key_grads[window_pos] + value_grads[window_pos], axis=1)
        for window_pos in window_range
    ]
    return (jnp.concatenate(out_parts, axis=1), jnp.concatenate(dq_parts, axis=1), window_terms)


def local(tokens, kv_weight, queries, out_grad, doc_lengths):
    row_count = tokens.shape[0]
    bal_index = lax.axis_index("bal")
    doc_ends = jnp.cumsum(doc_lengths[0])
    row_ids = jnp.arange(row_count, dtype=jnp.int32)
    own_pos = bal_index * row_count + row_ids
    own_doc = doc_index(doc_ends, own_pos)
    allowed_parts = []
    for distance in range(REACH, -1, -1):
        key_pos = (bal_index - distance) * row_count + row_ids
        key_doc = jnp.where(key_pos >= 0, doc_index(doc_ends, key_pos), -1)
        allowed_parts.append(
            (own_doc[:, None] == key_doc[None, :]) & (key_pos[None, :] <= own_pos[:, None])
        )
    full_weight = lax.all_gather(kv_weight, "fsdp", axis=0, tiled=True)
    kv_accum = jnp.dot(tokens, full_weight, preferred_element_type=jnp.float32)
    kv_rows = kv_accum.astype(jnp.bfloat16)
    earlier = [kv_rows]
    for distance in range(1, REACH + 1):
        earlier.append(from_behind(kv_rows, "bal", distance))
    kv_blocks = earlier[::-1]
    attn_out, grad_queries, window_terms = attend_rows(queries, kv_blocks, out_grad, allowed_parts)
    grad_terms = window_terms[::-1]
    grad_sum = grad_terms[0]
    for distance in range(1, REACH + 1):
        grad_sum = grad_sum + from_behind(
            grad_terms[distance].astype(jnp.bfloat16), "bal", -distance
        ).astype(jnp.float32)
    grad_kv = grad_sum.astype(jnp.bfloat16)
    grad_tokens = lax.dot_general(
        grad_kv, full_weight, (((1,), (1,)), ((), ())), preferred_element_type=jnp.float32
    ).astype(jnp.bfloat16)
    shard_sum = lax.psum_scatter(
        lax.dot_general(
            tokens, grad_kv, (((0,), (0,)), ((), ())), preferred_element_type=jnp.float32
        ).astype(jnp.bfloat16),
        "fsdp",
        scatter_dimension=0,
        tiled=True,
    )
    grad_weight = lax.psum(shard_sum, "bal").astype(jnp.float32)
    return (attn_out, grad_queries, grad_tokens, grad_weight)


def solution(mesh):
    placed = (
        P(("fsdp", "bal"), None),
        P("fsdp", None),
        P(("fsdp", "bal"), None),
        P(("fsdp", "bal"), None),
        P("fsdp", None),
    )
    one_plane = mesh.shape["bal"] == 8 and mesh.shape["fsdp"] == 4
    return jax.shard_map(
        plane_local if one_plane else local,
        mesh=mesh,
        in_specs=placed,
        out_specs=(
            P(("fsdp", "bal"), None),
            P(("fsdp", "bal"), None),
            P(("fsdp", "bal"), None),
            P("fsdp", None),
        ),
        check_vma=False,
    )
```

```python
import functools

import jax
import jax.numpy as jnp
from jax import lax
from jax.experimental import pallas as pl
from jax.experimental.pallas import tpu as pltpu
from jax.sharding import PartitionSpec as P

HEADS = 16
KV_HEADS = 4
HEAD_DIM = 128
REACH = 4

NEG_FILL = -1e30
F32 = jnp.float32
BF16 = jnp.bfloat16


def swap(value, axis, bit):
    count = lax.axis_size(axis)
    return lax.ppermute(value, axis, [(i, i ^ bit) for i in range(count)])


def dot(a, b, ca, cb):
    return lax.dot_general(a, b, (((ca,), (cb,)), ((), ())), preferred_element_type=F32)


def on_chip(shape, dtype=BF16):
    return pltpu.VMEM(shape, dtype)


def run(body, outs, scalars, arrays, scratch=(), room=16, aliases={}):
    arrays = [pltpu.with_memory_space_constraint(v, pltpu.VMEM) for v in arrays]
    return pl.pallas_call(
        body,
        out_shape=outs,
        in_specs=[pl.BlockSpec(memory_space=pltpu.SMEM)] * len(scalars)
        + [pl.BlockSpec(memory_space=pltpu.VMEM)] * len(arrays),
        out_specs=jax.tree.map(
            lambda _: pl.BlockSpec(memory_space=pltpu.VMEM), outs, is_leaf=lambda v: hasattr(v, "dtype")
        ),
        scratch_shapes=scratch,
        input_output_aliases=aliases,
        compiler_params=pltpu.CompilerParams(vmem_limit_bytes=room << 20),
        name=getattr(body, "func", body).__name__,
    )(*scalars, *arrays)


def column_of(chip, core):
    return core * (KV_HEADS * HEAD_DIM) + chip * HEAD_DIM


def quarter(z, r, size):
    return pl.ds(pl.multiple_of(jnp.bitwise_xor(z, r) * size, size), size)


def project_rows(z, xs, ws):
    size = ws[0].shape[0]
    total = None
    for r, w in enumerate(ws):
        x = jnp.concatenate([x[:, quarter(z, r, size)] for x in xs], axis=0)
        term = dot(x, w, 1, 0)
        total = term if total is None else total + term
    return total.astype(BF16)


def prep_kernel(ids, block, weight, x, w, x0):
    w[...] = weight[...]
    x0[...] = x[...]


def prepare(ids, block, weight, x):
    size = weight.shape[0]
    whole = pl.BlockSpec(x.shape, lambda i, ids, block: (0, 0))
    return pl.pallas_call(
        prep_kernel,
        out_shape=(on_chip((size, HEAD_DIM)), on_chip(x.shape)),
        grid_spec=pltpu.PrefetchScalarGridSpec(
            num_scalar_prefetch=2,
            grid=(1,),
            in_specs=[pl.BlockSpec((size, HEAD_DIM), lambda i, ids, block: (0, block[0])), whole],
            out_specs=[pl.BlockSpec(memory_space=pltpu.VMEM)] * 2,
        ),
        compiler_params=pltpu.CompilerParams(vmem_limit_bytes=16 << 20),
        name="prep_kernel",
    )(ids, block, *[pltpu.with_memory_space_constraint(v, pltpu.HBM) for v in (weight, x)])


def cut_kernel(x1, x2, top, low):
    half = top.shape[0]
    top[...] = x1[:half, :]
    low[...] = x2[half:, :]


def project_kernel(ids, *refs):
    *xs, w0, w1, w2, w3, out = refs
    out[...] = project_rows(ids[2], xs, (w0[...], w1[...], w2[...], w3[...]))


def order_kernel(ids, *refs):
    *xs, w0, w1, w2, w3, first, out = refs
    m, c, z = ids[0], ids[1], ids[2]
    chip_rows = first.shape[0] // 3
    rows = chip_rows // 2
    last = project_rows(z, xs, (w0[...], w1[...], w2[...], w3[...]))
    for r in range(4):
        part = first[r * chip_rows : (r + 1) * chip_rows, :] if r < 3 else last
        chip = jnp.bitwise_xor(m, r)
        out[shard_rows(2 * chip + c, rows), :] = part[:rows]
        out[shard_rows(2 * chip + 1 - c, rows), :] = part[rows:]


def shard_rows(shard, rows, count=1):
    return pl.ds(pl.multiple_of(shard * rows, rows), rows * count)


def cut_heads_kernel(ids, *refs):
    for r in range(4):
        refs[8 + r][0] = refs[2 * r][...]
        refs[8 + r][1] = refs[2 * r + 1][...]


def cut_heads(ids, queries, out_grad):
    rows = queries.shape[0]
    width = queries.shape[1] // KV_HEADS
    both = [pltpu.with_memory_space_constraint(v, pltpu.HBM) for v in (queries, out_grad)]
    return pl.pallas_call(
        cut_heads_kernel,
        out_shape=(on_chip((2, rows, width)),) * 4,
        grid_spec=pltpu.PrefetchScalarGridSpec(
            num_scalar_prefetch=1,
            grid=(1,),
            in_specs=[
                pl.BlockSpec((rows, width), lambda i, ids, r=r: (0, jnp.bitwise_xor(ids[0], r)))
                for r in (0, 0, 1, 1, 2, 2, 3, 3)
            ],
            out_specs=[pl.BlockSpec(memory_space=pltpu.VMEM)] * 4,
        ),
        compiler_params=pltpu.CompilerParams(vmem_limit_bytes=16 << 20),
        name="cut_heads_kernel",
    )(ids, *(both * 4))


def attend_kernel(rels, docs, first_call, last_call, ids, lens, *refs):
    count = len(rels)
    m, c = ids[0], ids[1]
    is_key = c == 0
    if first_call:
        mine, got, *refs = refs
        qgs, outs, (dk, dv, key, val) = refs[:count], refs[count : 2 * count], refs[2 * count :]
        key[...] = jnp.where(is_key, mine[...], got[...])
        val[...] = jnp.where(is_key, got[...], mine[...])
        dk[...] = jnp.zeros_like(dk)
        dv[...] = jnp.zeros_like(dv)
    elif last_call:
        dk, dv, key, val, *refs = refs
        qgs, outs, (own, keep, send) = refs[:count], refs[count : 2 * count], refs[2 * count :]
    else:
        _, _, key, val, *refs = refs
        qgs, outs, (dk, dv) = refs[:count], refs[count : 2 * count], refs[2 * count :]
    rows = qgs[0].shape[1]
    heads = HEADS // KV_HEADS
    inv = HEAD_DIM ** (-0.5)

    def body(i, shard, begin, shards):
        span = shard_rows(begin, rows, shards)
        size = shards * rows
        kpos = lax.broadcasted_iota(jnp.int32, (size, 1), 0) + begin * rows
        qpos = lax.broadcasted_iota(jnp.int32, (1, rows), 1) + shard * rows
        kdoc = jnp.zeros_like(kpos)
        qdoc = jnp.zeros_like(qpos)
        end = jnp.int32(0)
        for k in range(docs):
            end = end + lens[0, k]
            kdoc = kdoc + (kpos >= end).astype(jnp.int32)
            qdoc = qdoc + (qpos >= end).astype(jnp.int32)
        bias = jnp.where((kdoc == qdoc) & (kpos <= qpos), 0.0, NEG_FILL)
        bias = jnp.concatenate([bias] * heads, axis=1)
        cols = [slice(h * HEAD_DIM, (h + 1) * HEAD_DIM) for h in range(heads)]
        k, v = key[span, :], val[span, :]
        q = jnp.concatenate([qgs[i][0, :, at] for at in cols], axis=0)
        g = jnp.concatenate([qgs[i][1, :, at] for at in cols], axis=0)
        s = dot(k, q, 1, 1) * inv + bias
        p = jnp.exp(s - jnp.max(s, axis=0, keepdims=True))
        p = p * (1.0 / jnp.sum(p, axis=0, keepdims=True))
        low = p.astype(BF16)
        out = dot(low, v, 0, 0).astype(BF16)
        delta = jnp.sum(out.astype(F32).T * g.astype(F32).T, axis=0, keepdims=True)
        ds = (p * (dot(v, g, 1, 1) - delta)).astype(BF16)
        dq = (dot(ds, k, 0, 0) * inv).astype(BF16)
        dk[span, :] = dk[span, :] + dot(ds, q, 1, 0) * inv
        dv[span, :] = dv[span, :] + dot(low, g, 1, 0)
        for h, at in enumerate(cols):
            outs[i][0, :, at] = out[h * rows : (h + 1) * rows]
            outs[i][1, :, at] = dq[h * rows : (h + 1) * rows]

    for i, r in enumerate(rels):
        chip = jnp.bitwise_xor(m, r)
        shard = 2 * chip + c

        @pl.when(chip == 0)
        def _():
            body(i, shard, 0, 2)

        @pl.when(chip > 0)
        def _():
            body(i, shard, jnp.maximum(shard - REACH, 0), REACH + 1)

    if last_call:
        own[...] = jnp.where(is_key, dk[...], dv[...])
        size = own.shape[0]
        send[:size, :] = jnp.where(is_key, dv[...], dk[...]).astype(BF16)
        for chip in range(4):
            at = slice(chip * rows, (chip + 1) * rows)
            mine, theirs = shard_rows(2 * chip + c, rows), shard_rows(2 * chip + 1 - c, rows)
            keep[at, :] = jnp.where(is_key, dv[mine, :], dk[mine, :])
            send[size + chip * rows : size + (chip + 1) * rows, :] = own[theirs, :].astype(BF16)


def attend(rels, ids, lens, state, qgs, last=False):
    first = len(state) == 2
    total = (state[0].shape[0], HEAD_DIM)
    sums = (on_chip(total, F32), on_chip(total, F32))
    if last:
        part = total[0] // 2
        sums = (on_chip(total, F32), on_chip((part, HEAD_DIM), F32), on_chip((total[0] + part, HEAD_DIM)))
    if first:
        sums = sums + (on_chip(total), on_chip(total))
    count = len(rels)
    results = run(
        functools.partial(attend_kernel, rels, lens.shape[1], first, last),
        tuple(on_chip(v.shape) for v in qgs) + sums,
        (ids, lens),
        (*state, *qgs),
        room=24,
        aliases={} if first or last else {2: count, 3: count + 1},
    )
    outs, state_out = results[:count], results[count:]
    return outs, (state_out if first or last else (*state_out, *state[2:]))


def place_kernel(ids, p0, p1, p2, p3, out, dq):
    width = p0.shape[2]
    for r, part in enumerate((p0, p1, p2, p3)):
        cols = quarter(ids[0], r, width)
        out[:, cols] = part[0]
        dq[:, cols] = part[1]


def weight_block(z, r, g_t, xs, size):
    x = jnp.concatenate([x[:, quarter(z, r, size)] for x in xs], axis=0)
    return dot(g_t, x, 1, 0).T


def weight_kernel(ids, mine, got, *refs):
    *xs, keep, send1, send2, send3, g_t = refs
    m, c, z = ids[0], ids[1], ids[2]
    rows = g_t.shape[1] // 8
    for r in range(4):
        chip = jnp.bitwise_xor(m, r)
        for e, core in enumerate((c, 1 - c)):
            span = shard_rows(2 * chip + core, rows)
            g = (mine[span, :] + got[span, :].astype(F32)).astype(BF16)
            g_t[:, (2 * r + e) * rows : (2 * r + e + 1) * rows] = g.T
    for r, send in ((3, send3), (2, send2), (1, send1)):
        send[...] = weight_block(z, r, g_t[...], xs, send.shape[0]).astype(BF16)
    keep[...] = weight_block(z, 0, g_t[...], xs, keep.shape[0])


def fold_kernel(keep, got, now, later):
    now[...] = keep[0] + got[0].astype(F32)
    later[...] = (keep[1] + got[1].astype(F32)).astype(BF16)


def add_kernel(keep, got, out):
    out[...] = keep[...] + got[...].astype(F32)


def last_kernel(keep, got1, got2, out):
    out[...] = (keep[...] + (got1[...].astype(F32) + got2[...].astype(F32))).astype(BF16)


def assemble_kernel(ids, *refs):
    m, c = ids[0], ids[1]
    out = refs[-1]
    for side, core in enumerate((c, 1 - c)):
        for r in range(4):
            col = pl.multiple_of(column_of(jnp.bitwise_xor(m, r), core), HEAD_DIM)
            out[:, pl.ds(col, HEAD_DIM)] = refs[4 * side + r][...].astype(F32)


def token_kernel(ids, mine, kept, got, w0, w1, w2, w3, u0, u1, u2, u3,
                 send_a, send_b, keep_a, keep_b):
    m, c = ids[0], ids[1]
    size = mine.shape[0]
    rows = size // 8
    parts = []
    for r in range(4):
        chip = jnp.bitwise_xor(m, r)
        span = shard_rows(2 * chip + c, rows)
        own = mine[span, :] + got[span, :].astype(F32)
        oth = kept[shard_rows(chip, rows), :] + got[shard_rows(8 + chip, rows), :].astype(F32)
        parts.append(jnp.concatenate([own, oth], axis=1).astype(BF16))
    g = jnp.concatenate(parts, axis=0)
    ws = (w0[...], w1[...], w2[...], w3[...])
    us = (u0[...], u1[...], u2[...], u3[...])
    size = w0.shape[0]
    for i in range(4):
        w = jnp.concatenate([ws[i], us[i]], axis=1)
        t = dot(g, w, 1, 1)
        at = slice((i % 2) * size, (i % 2 + 1) * size)
        send, keep, away = (send_a, keep_a, (1, 3)) if i < 2 else (send_b, keep_b, (2, 3))
        home = [r for r in range(4) if r not in away]
        for k in range(2):
            send[k, :, at] = t[away[k] * rows : (away[k] + 1) * rows].astype(BF16)
            keep[k, :, at] = t[home[k] * rows : (home[k] + 1) * rows]


def fold_both_kernel(keep_a, got_a, keep_b, got_b, a, a_send, b, b_send):
    fold_kernel(keep_a, got_a, a, a_send)
    fold_kernel(keep_b, got_b, b, b_send)


def token_last_kernel(ids, a, got_a, b, got_b, out):
    size = out.shape[1] // 4
    for i in range(4):
        now, got = (a, got_a) if i < 2 else (b, got_b)
        at = slice((i % 2) * size, (i % 2 + 1) * size)
        out[:, quarter(ids[2], i, size)] = (now[:, at] + got[:, at].astype(F32)).astype(BF16)


def plane_local(tokens, kv_weight, queries, out_grad, doc_lengths):
    rows, width = tokens.shape
    size = kv_weight.shape[0]
    m, c = lax.axis_index("bal") // 2, lax.axis_index("bal") % 2
    ids = jnp.stack([m, c, lax.axis_index("fsdp")]).astype(jnp.int32)
    pair = lambda v: swap(v, "bal", 1)
    near = lambda v: swap(v, "bal", 2)
    far = lambda v: swap(v, "bal", 4)
    cross = lambda v: swap(v, "bal", 6)

    x1, x2 = near(tokens), far(tokens)
    block = (column_of(m, c) // HEAD_DIM).astype(jnp.int32).reshape(1)
    w0, x0 = prepare(ids, block, kv_weight, tokens)
    w2, w1 = swap(w0, "fsdp", 2), swap(w0, "fsdp", 1)
    x1, x2, w1, w2 = lax.optimization_barrier((x1, x2, w1, w2))
    w3 = swap(w2, "fsdp", 1)
    ws = (w0, w1, w2, w3)
    half = on_chip((rows // 2, width))
    p0, *away = cut_heads(ids, queries, out_grad)
    x1, x2, *away = lax.optimization_barrier((x1, x2, *away))
    p1, p2, p3 = away
    top, low = run(cut_kernel, (half, half), (), (x1, x2))
    x3 = [far(top), near(low)]
    flip = lambda vs: [pair(v) for v in vs]
    early = (x0, pair(x0), x1, pair(x1), x2, pair(x2))
    p1, p2 = near(p1), far(p2)
    first = run(project_kernel, on_chip((6 * rows, HEAD_DIM)), (ids,), early + ws)
    *x3, first = lax.optimization_barrier((*x3, first))
    us = tuple(flip(ws))
    late = (*x3, *flip(x3))
    xs = early + late
    p1, p2, p3, first = lax.optimization_barrier((p1, p2, p3, first))
    mine = run(order_kernel, on_chip((8 * rows, HEAD_DIM)), (ids,), late + ws + (first,))
    p3 = cross(p3)
    got = pair(mine)
    (o0,), state = attend((0,), ids, doc_lengths, (mine, got), (p0,))
    p1, p2, *state = lax.optimization_barrier((p1, p2, *state))
    (o1, o2), state = attend((1, 2), ids, doc_lengths, state, (p1, p2))
    o1, o2 = near(o1), far(o2)
    p3, *state = lax.optimization_barrier((p3, *state))
    (o3,), (g_mine, g_keep, g_send) = attend((3,), ids, doc_lengths, state, (p3,), True)
    g_send, us = lax.optimization_barrier((g_send, us))
    g_got = pair(g_send)
    o3 = cross(o3)

    third = on_chip((size, HEAD_DIM))
    half = (rows, width // 2)
    send_a, send_b, keep_a, keep_b = run(
        token_kernel,
        (on_chip((2, *half)), on_chip((2, *half)), on_chip((2, *half), F32), on_chip((2, *half), F32)),
        (ids,),
        (g_mine, g_keep, g_got) + ws + us,
    )
    got_a, got_b = near(send_a), far(send_b)
    keep, *sends = run(
        weight_kernel,
        (on_chip((size, HEAD_DIM), F32), third, third, third),
        (ids,),
        (g_mine, g_got) + xs,
        scratch=[pltpu.VMEM((HEAD_DIM, 8 * rows), BF16)],
    )
    gots = [swap(v, "fsdp", bit) for v, bit in zip(sends, (1, 2, 3))]
    keep = run(add_kernel, on_chip((size, HEAD_DIM), F32), (), (keep, gots[0]))
    mine = run(last_kernel, on_chip((size, HEAD_DIM)), (), (keep, *gots[1:]))
    got_a, got_b, mine = lax.optimization_barrier((got_a, got_b, mine))
    fold = (on_chip(half, F32), on_chip(half))
    a, a_send, b, b_send = run(fold_both_kernel, fold + fold, (), (keep_a, got_a, keep_b, got_b))
    got_a, got_b = far(a_send), near(b_send)
    like = jax.ShapeDtypeStruct(queries.shape, BF16)
    mine = [mine, near(mine), far(mine), cross(mine)]
    mine[1], o1, o2, o3 = lax.optimization_barrier((mine[1], o1, o2, o3))
    attn_out, grad_queries = run(place_kernel, (like, like), (ids,), (o0, o1, o2, o3))
    mine[2], mine[3], attn_out, grad_queries = lax.optimization_barrier((mine[2], mine[3], attn_out, grad_queries))
    theirs = [pair(v) for v in mine]
    grad_weight = run(
        assemble_kernel,
        jax.ShapeDtypeStruct((size, kv_weight.shape[1]), F32),
        (ids,),
        mine + theirs,
    )
    grad_tokens = run(
        token_last_kernel, jax.ShapeDtypeStruct(tokens.shape, BF16), (ids,), (a, got_a, b, got_b)
    )
    return attn_out, grad_queries, grad_tokens, grad_weight


def from_behind(value, axis, steps):
    count = lax.axis_size(axis)
    initial, last = (max(0, -steps), min(count, count - steps))
    return lax.ppermute(value, axis, [(source, source + steps) for source in range(initial, last)])


def doc_index(doc_ends, positions):
    return jnp.sum((doc_ends[None, :] <= positions[:, None]).astype(jnp.int32), axis=1)


def score_tile(q_group, key_block, mask_block, inv_root):
    raw_scores = (
        jnp.einsum("qhd,kd->hqk", q_group, key_block, preferred_element_type=jnp.float32) * inv_root
    )
    return jnp.where(mask_block[None], raw_scores, NEG_FILL)


def value_tile(prob_tile, value_block):
    return jnp.einsum("hqk,kd->qhd", prob_tile, value_block, preferred_element_type=jnp.float32)


def dprob_tile(grad_group, value_block):
    return jnp.einsum("qhd,kd->hqk", grad_group, value_block, preferred_element_type=jnp.float32)


def query_tile(dscore_tile, key_block):
    return jnp.einsum("hqk,kd->qhd", dscore_tile, key_block, preferred_element_type=jnp.float32)


def key_tile(dscore_tile, q_group, inv_root):
    return (
        jnp.einsum("hqk,qhd->kd", dscore_tile, q_group, preferred_element_type=jnp.float32)
        * inv_root
    )


def value_grad_tile(prob_tile, grad_group):
    return jnp.einsum("hqk,qhd->kd", prob_tile, grad_group, preferred_element_type=jnp.float32)


def attend_rows(q_rows, kv_blocks, grad_rows, allowed_parts):
    row_count = q_rows.shape[0]
    key_rows = kv_blocks[0].shape[0]
    group_size = HEADS // KV_HEADS
    inv_root = HEAD_DIM ** (-0.5)
    window_range = list(range(len(kv_blocks)))
    row_shape = (row_count, group_size, HEAD_DIM)
    out_parts = []
    dq_parts = []
    key_grads = [[] for window_pos in window_range]
    value_grads = [[] for window_pos in window_range]
    for head_group in range(KV_HEADS):
        col_start = head_group * group_size * HEAD_DIM
        col_stop = col_start + group_size * HEAD_DIM
        val_start = (KV_HEADS + head_group) * HEAD_DIM
        q_group = q_rows[:, col_start:col_stop].reshape(row_shape)
        grad_group = grad_rows[:, col_start:col_stop].reshape(row_shape)
        key_list = [
            piece[:, head_group * HEAD_DIM : (head_group + 1) * HEAD_DIM] for piece in kv_blocks
        ]
        value_list = [piece[:, val_start : val_start + HEAD_DIM] for piece in kv_blocks]
        score_tiles = [
            score_tile(q_group, key_list[window_pos], allowed_parts[window_pos], inv_root)
            for window_pos in window_range
        ]
        scores = jnp.concatenate(score_tiles, axis=2)
        row_max = jnp.max(scores, axis=-1, keepdims=True)
        exp_shift = jnp.exp(scores - row_max)
        prob_full = exp_shift / jnp.sum(exp_shift, axis=-1, keepdims=True)
        prob_low = prob_full.astype(jnp.bfloat16)
        prob_tiles = [
            prob_low[:, :, window_pos * key_rows : (window_pos + 1) * key_rows]
            for window_pos in window_range
        ]
        out_accum = jnp.zeros(row_shape, jnp.float32)
        for window_pos in window_range:
            out_accum = out_accum + value_tile(prob_tiles[window_pos], value_list[window_pos])
        out_group = out_accum.astype(jnp.bfloat16)
        row_delta = jnp.sum(grad_group.astype(jnp.float32) * out_group.astype(jnp.float32), axis=-1)
        dprob_tiles = [
            dprob_tile(grad_group, value_list[window_pos]) for window_pos in window_range
        ]
        dprobs = jnp.concatenate(dprob_tiles, axis=2)
        dscores = (prob_full * (dprobs - row_delta.T[:, :, None])).astype(jnp.bfloat16)
        dq_accum = jnp.zeros(row_shape, jnp.float32)
        for window_pos in window_range:
            dscore_piece = dscores[:, :, window_pos * key_rows : (window_pos + 1) * key_rows]
            dq_accum = dq_accum + query_tile(dscore_piece, key_list[window_pos])
            key_grads[window_pos].append(key_tile(dscore_piece, q_group, inv_root))
            value_grads[window_pos].append(value_grad_tile(prob_tiles[window_pos], grad_group))
        dq_group = (dq_accum * inv_root).astype(jnp.bfloat16)
        out_parts.append(out_group.reshape(row_count, group_size * HEAD_DIM))
        dq_parts.append(dq_group.reshape(row_count, group_size * HEAD_DIM))
    window_terms = [
        jnp.concatenate(key_grads[window_pos] + value_grads[window_pos], axis=1)
        for window_pos in window_range
    ]
    return (jnp.concatenate(out_parts, axis=1), jnp.concatenate(dq_parts, axis=1), window_terms)


def local(tokens, kv_weight, queries, out_grad, doc_lengths):
    row_count = tokens.shape[0]
    bal_index = lax.axis_index("bal")
    doc_ends = jnp.cumsum(doc_lengths[0])
    row_ids = jnp.arange(row_count, dtype=jnp.int32)
    own_pos = bal_index * row_count + row_ids
    own_doc = doc_index(doc_ends, own_pos)
    allowed_parts = []
    for distance in range(REACH, -1, -1):
        key_pos = (bal_index - distance) * row_count + row_ids
        key_doc = jnp.where(key_pos >= 0, doc_index(doc_ends, key_pos), -1)
        allowed_parts.append(
            (own_doc[:, None] == key_doc[None, :]) & (key_pos[None, :] <= own_pos[:, None])
        )
    full_weight = lax.all_gather(kv_weight, "fsdp", axis=0, tiled=True)
    kv_accum = jnp.dot(tokens, full_weight, preferred_element_type=jnp.float32)
    kv_rows = kv_accum.astype(jnp.bfloat16)
    earlier = [kv_rows]
    for distance in range(1, REACH + 1):
        earlier.append(from_behind(kv_rows, "bal", distance))
    kv_blocks = earlier[::-1]
    attn_out, grad_queries, window_terms = attend_rows(queries, kv_blocks, out_grad, allowed_parts)
    grad_terms = window_terms[::-1]
    grad_sum = grad_terms[0]
    for distance in range(1, REACH + 1):
        grad_sum = grad_sum + from_behind(
            grad_terms[distance].astype(jnp.bfloat16), "bal", -distance
        ).astype(jnp.float32)
    grad_kv = grad_sum.astype(jnp.bfloat16)
    grad_tokens = lax.dot_general(
        grad_kv, full_weight, (((1,), (1,)), ((), ())), preferred_element_type=jnp.float32
    ).astype(jnp.bfloat16)
    shard_sum = lax.psum_scatter(
        lax.dot_general(
            tokens, grad_kv, (((0,), (0,)), ((), ())), preferred_element_type=jnp.float32
        ).astype(jnp.bfloat16),
        "fsdp",
        scatter_dimension=0,
        tiled=True,
    )
    grad_weight = lax.psum(shard_sum, "bal").astype(jnp.float32)
    return (attn_out, grad_queries, grad_tokens, grad_weight)


def solution(mesh):
    placed = (
        P(("fsdp", "bal"), None),
        P("fsdp", None),
        P(("fsdp", "bal"), None),
        P(("fsdp", "bal"), None),
        P("fsdp", None),
    )
    one_plane = mesh.shape["bal"] == 8 and mesh.shape["fsdp"] == 4
    return jax.shard_map(
        plane_local if one_plane else local,
        mesh=mesh,
        in_specs=placed,
        out_specs=(
            P(("fsdp", "bal"), None),
            P(("fsdp", "bal"), None),
            P(("fsdp", "bal"), None),
            P("fsdp", None),
        ),
        check_vma=False,
    )
```

```python
import functools

import jax
import jax.numpy as jnp
from jax import lax
from jax.experimental import pallas as pl
from jax.experimental.pallas import tpu as pltpu
from jax.sharding import PartitionSpec as P

HEADS = 16
KV_HEADS = 4
HEAD_DIM = 128
REACH = 4

NEG_FILL = -1e30
F32 = jnp.float32
BF16 = jnp.bfloat16


def swap(value, axis, bit):
    count = lax.axis_size(axis)
    return lax.ppermute(value, axis, [(i, i ^ bit) for i in range(count)])


def dot(a, b, ca, cb):
    return lax.dot_general(a, b, (((ca,), (cb,)), ((), ())), preferred_element_type=F32)


def on_chip(shape, dtype=BF16):
    return pltpu.VMEM(shape, dtype)


def run(body, outs, scalars, arrays, scratch=(), room=16, aliases={}):
    arrays = [pltpu.with_memory_space_constraint(v, pltpu.VMEM) for v in arrays]
    return pl.pallas_call(
        body,
        out_shape=outs,
        in_specs=[pl.BlockSpec(memory_space=pltpu.SMEM)] * len(scalars)
        + [pl.BlockSpec(memory_space=pltpu.VMEM)] * len(arrays),
        out_specs=jax.tree.map(
            lambda _: pl.BlockSpec(memory_space=pltpu.VMEM), outs, is_leaf=lambda v: hasattr(v, "dtype")
        ),
        scratch_shapes=scratch,
        input_output_aliases=aliases,
        compiler_params=pltpu.CompilerParams(vmem_limit_bytes=room << 20),
        name=getattr(body, "func", body).__name__,
    )(*scalars, *arrays)


def column_of(chip, core):
    return core * (KV_HEADS * HEAD_DIM) + chip * HEAD_DIM


def quarter(z, r, size):
    return pl.ds(pl.multiple_of(jnp.bitwise_xor(z, r) * size, size), size)


def project_rows(z, xs, ws):
    size = ws[0].shape[0]
    total = None
    for r, w in enumerate(ws):
        x = jnp.concatenate([x[:, quarter(z, r, size)] for x in xs], axis=0)
        term = dot(x, w, 1, 0)
        total = term if total is None else total + term
    return total.astype(BF16)


def prep_kernel(ids, block, weight, x, w, x0):
    w[...] = weight[...]
    x0[...] = x[...]


def prepare(ids, block, weight, x):
    size = weight.shape[0]
    whole = pl.BlockSpec(x.shape, lambda i, ids, block: (0, 0))
    return pl.pallas_call(
        prep_kernel,
        out_shape=(on_chip((size, HEAD_DIM)), on_chip(x.shape)),
        grid_spec=pltpu.PrefetchScalarGridSpec(
            num_scalar_prefetch=2,
            grid=(1,),
            in_specs=[pl.BlockSpec((size, HEAD_DIM), lambda i, ids, block: (0, block[0])), whole],
            out_specs=[pl.BlockSpec(memory_space=pltpu.VMEM)] * 2,
        ),
        compiler_params=pltpu.CompilerParams(vmem_limit_bytes=16 << 20),
        name="prep_kernel",
    )(ids, block, *[pltpu.with_memory_space_constraint(v, pltpu.HBM) for v in (weight, x)])


def cut_kernel(x1, x2, top, low):
    half = top.shape[0]
    top[...] = x1[:half, :]
    low[...] = x2[half:, :]


def project_kernel(ids, *refs):
    *xs, w0, w1, w2, w3, out = refs
    out[...] = project_rows(ids[2], xs, (w0[...], w1[...], w2[...], w3[...]))


def order_kernel(ids, *refs):
    *xs, w0, w1, w2, w3, first, out = refs
    m, c, z = ids[0], ids[1], ids[2]
    chip_rows = first.shape[0] // 3
    rows = chip_rows // 2
    last = project_rows(z, xs, (w0[...], w1[...], w2[...], w3[...]))
    for r in range(4):
        part = first[r * chip_rows : (r + 1) * chip_rows, :] if r < 3 else last
        chip = jnp.bitwise_xor(m, r)
        out[shard_rows(2 * chip + c, rows), :] = part[:rows]
        out[shard_rows(2 * chip + 1 - c, rows), :] = part[rows:]


def shard_rows(shard, rows, count=1):
    return pl.ds(pl.multiple_of(shard * rows, rows), rows * count)


def cut_heads_kernel(ids, *refs):
    for r in range(4):
        refs[8 + r][0] = refs[2 * r][...]
        refs[8 + r][1] = refs[2 * r + 1][...]


def cut_heads(ids, queries, out_grad):
    rows = queries.shape[0]
    width = queries.shape[1] // KV_HEADS
    both = [pltpu.with_memory_space_constraint(v, pltpu.HBM) for v in (queries, out_grad)]
    return pl.pallas_call(
        cut_heads_kernel,
        out_shape=(on_chip((2, rows, width)),) * 4,
        grid_spec=pltpu.PrefetchScalarGridSpec(
            num_scalar_prefetch=1,
            grid=(1,),
            in_specs=[
                pl.BlockSpec((rows, width), lambda i, ids, r=r: (0, jnp.bitwise_xor(ids[0], r)))
                for r in (0, 0, 1, 1, 2, 2, 3, 3)
            ],
            out_specs=[pl.BlockSpec(memory_space=pltpu.VMEM)] * 4,
        ),
        compiler_params=pltpu.CompilerParams(vmem_limit_bytes=16 << 20),
        name="cut_heads_kernel",
    )(ids, *(both * 4))


def attend_kernel(rels, docs, first_call, last_call, ids, lens, *refs):
    count = len(rels)
    m, c = ids[0], ids[1]
    is_key = c == 0
    if first_call:
        mine, got, *refs = refs
        qgs, outs, (dk, dv, key, val) = refs[:count], refs[count : 2 * count], refs[2 * count :]
        key[...] = jnp.where(is_key, mine[...], got[...])
        val[...] = jnp.where(is_key, got[...], mine[...])
        dk[...] = jnp.zeros_like(dk)
        dv[...] = jnp.zeros_like(dv)
    elif last_call:
        dk, dv, key, val, *refs = refs
        qgs, outs, (own, keep, send) = refs[:count], refs[count : 2 * count], refs[2 * count :]
    else:
        _, _, key, val, *refs = refs
        qgs, outs, (dk, dv) = refs[:count], refs[count : 2 * count], refs[2 * count :]
    rows = qgs[0].shape[1]
    heads = HEADS // KV_HEADS
    inv = HEAD_DIM ** (-0.5)

    def body(i, shard, begin, shards):
        span = shard_rows(begin, rows, shards)
        size = shards * rows
        kpos = lax.broadcasted_iota(jnp.int32, (size, 1), 0) + begin * rows
        qpos = lax.broadcasted_iota(jnp.int32, (1, rows), 1) + shard * rows
        kdoc = jnp.zeros_like(kpos)
        qdoc = jnp.zeros_like(qpos)
        end = jnp.int32(0)
        for k in range(docs):
            end = end + lens[0, k]
            kdoc = kdoc + (kpos >= end).astype(jnp.int32)
            qdoc = qdoc + (qpos >= end).astype(jnp.int32)
        bias = jnp.where((kdoc == qdoc) & (kpos <= qpos), 0.0, NEG_FILL)
        bias = jnp.concatenate([bias] * heads, axis=1)
        cols = [slice(h * HEAD_DIM, (h + 1) * HEAD_DIM) for h in range(heads)]
        k, v = key[span, :], val[span, :]
        q = jnp.concatenate([qgs[i][0, :, at] for at in cols], axis=0)
        g = jnp.concatenate([qgs[i][1, :, at] for at in cols], axis=0)
        s = dot(k, q, 1, 1) * inv + bias
        p = jnp.exp(s - jnp.max(s, axis=0, keepdims=True))
        p = p * (1.0 / jnp.sum(p, axis=0, keepdims=True))
        low = p.astype(BF16)
        out = dot(low, v, 0, 0).astype(BF16)
        delta = jnp.sum(out.astype(F32).T * g.astype(F32).T, axis=0, keepdims=True)
        ds = (p * (dot(v, g, 1, 1) - delta)).astype(BF16)
        dq = (dot(ds, k, 0, 0) * inv).astype(BF16)
        dk[span, :] = dk[span, :] + dot(ds, q, 1, 0) * inv
        dv[span, :] = dv[span, :] + dot(low, g, 1, 0)
        for h, at in enumerate(cols):
            outs[i][0, :, at] = out[h * rows : (h + 1) * rows]
            outs[i][1, :, at] = dq[h * rows : (h + 1) * rows]

    for i, r in enumerate(rels):
        chip = jnp.bitwise_xor(m, r)
        shard = 2 * chip + c

        @pl.when(chip == 0)
        def _():
            body(i, shard, 0, 2)

        @pl.when(chip > 0)
        def _():
            body(i, shard, jnp.maximum(shard - REACH, 0), REACH + 1)

    if last_call:
        own[...] = jnp.where(is_key, dk[...], dv[...])
        size = own.shape[0]
        send[:size, :] = jnp.where(is_key, dv[...], dk[...]).astype(BF16)
        for chip in range(4):
            at = slice(chip * rows, (chip + 1) * rows)
            mine, theirs = shard_rows(2 * chip + c, rows), shard_rows(2 * chip + 1 - c, rows)
            keep[at, :] = jnp.where(is_key, dv[mine, :], dk[mine, :])
            send[size + chip * rows : size + (chip + 1) * rows, :] = own[theirs, :].astype(BF16)


def attend(rels, ids, lens, state, qgs, last=False):
    first = len(state) == 2
    total = (state[0].shape[0], HEAD_DIM)
    sums = (on_chip(total, F32), on_chip(total, F32))
    if last:
        part = total[0] // 2
        sums = (on_chip(total, F32), on_chip((part, HEAD_DIM), F32), on_chip((total[0] + part, HEAD_DIM)))
    if first:
        sums = sums + (on_chip(total), on_chip(total))
    count = len(rels)
    results = run(
        functools.partial(attend_kernel, rels, lens.shape[1], first, last),
        tuple(on_chip(v.shape) for v in qgs) + sums,
        (ids, lens),
        (*state, *qgs),
        room=24,
        aliases={} if first or last else {2: count, 3: count + 1},
    )
    outs, state_out = results[:count], results[count:]
    return outs, (state_out if first or last else (*state_out, *state[2:]))


def place_kernel(ids, p0, p1, p2, p3, out, dq):
    width = p0.shape[2]
    for r, part in enumerate((p0, p1, p2, p3)):
        cols = quarter(ids[0], r, width)
        out[:, cols] = part[0]
        dq[:, cols] = part[1]


def weight_block(z, r, g_t, xs, size):
    x = jnp.concatenate([x[:, quarter(z, r, size)] for x in xs], axis=0)
    return dot(g_t, x, 1, 0).T


def weight_kernel(ids, mine, got, *refs):
    *xs, keep, send1, send2, send3, g_t = refs
    m, c, z = ids[0], ids[1], ids[2]
    rows = g_t.shape[1] // 8
    for r in range(4):
        chip = jnp.bitwise_xor(m, r)
        for e, core in enumerate((c, 1 - c)):
            span = shard_rows(2 * chip + core, rows)
            g = (mine[span, :] + got[span, :].astype(F32)).astype(BF16)
            g_t[:, (2 * r + e) * rows : (2 * r + e + 1) * rows] = g.T
    for r, send in ((3, send3), (2, send2), (1, send1)):
        send[...] = weight_block(z, r, g_t[...], xs, send.shape[0]).astype(BF16)
    keep[...] = weight_block(z, 0, g_t[...], xs, keep.shape[0])


def fold_kernel(keep, got, now, later):
    now[...] = keep[0] + got[0].astype(F32)
    later[...] = (keep[1] + got[1].astype(F32)).astype(BF16)


def add_kernel(keep, got, out):
    out[...] = keep[...] + got[...].astype(F32)


def last_kernel(keep, got1, got2, out):
    out[...] = (keep[...] + (got1[...].astype(F32) + got2[...].astype(F32))).astype(BF16)


def assemble_kernel(ids, *refs):
    m, c = ids[0], ids[1]
    out = refs[-1]
    for side, core in enumerate((c, 1 - c)):
        for r in range(4):
            col = pl.multiple_of(column_of(jnp.bitwise_xor(m, r), core), HEAD_DIM)
            out[:, pl.ds(col, HEAD_DIM)] = refs[4 * side + r][...].astype(F32)


def token_kernel(ids, mine, kept, got, w0, w1, w2, w3, u0, u1, u2, u3,
                 send_a, send_b, keep_a, keep_b):
    m, c = ids[0], ids[1]
    size = mine.shape[0]
    rows = size // 8
    parts = []
    for r in range(4):
        chip = jnp.bitwise_xor(m, r)
        span = shard_rows(2 * chip + c, rows)
        own = mine[span, :] + got[span, :].astype(F32)
        oth = kept[shard_rows(chip, rows), :] + got[shard_rows(8 + chip, rows), :].astype(F32)
        parts.append(jnp.concatenate([own, oth], axis=1).astype(BF16))
    g = jnp.concatenate(parts, axis=0)
    ws = (w0[...], w1[...], w2[...], w3[...])
    us = (u0[...], u1[...], u2[...], u3[...])
    size = w0.shape[0]
    for i in range(4):
        w = jnp.concatenate([ws[i], us[i]], axis=1)
        t = dot(g, w, 1, 1)
        at = slice((i % 2) * size, (i % 2 + 1) * size)
        send, keep, away = (send_a, keep_a, (1, 3)) if i < 2 else (send_b, keep_b, (2, 3))
        home = [r for r in range(4) if r not in away]
        for k in range(2):
            send[k, :, at] = t[away[k] * rows : (away[k] + 1) * rows].astype(BF16)
            keep[k, :, at] = t[home[k] * rows : (home[k] + 1) * rows]


def fold_both_kernel(keep_a, got_a, keep_b, got_b, a, a_send, b, b_send):
    fold_kernel(keep_a, got_a, a, a_send)
    fold_kernel(keep_b, got_b, b, b_send)


def token_last_kernel(ids, a, got_a, b, got_b, out):
    size = out.shape[1] // 4
    for i in range(4):
        now, got = (a, got_a) if i < 2 else (b, got_b)
        at = slice((i % 2) * size, (i % 2 + 1) * size)
        out[:, quarter(ids[2], i, size)] = (now[:, at] + got[:, at].astype(F32)).astype(BF16)


def final_kernel(ids, *refs):
    *blocks, a, got_a, b, got_b, weight_out, token_out = refs
    token_last_kernel(ids, a, got_a, b, got_b, token_out)
    assemble_kernel(ids, *blocks, weight_out)


def plane_local(tokens, kv_weight, queries, out_grad, doc_lengths):
    rows, width = tokens.shape
    size = kv_weight.shape[0]
    m, c = lax.axis_index("bal") // 2, lax.axis_index("bal") % 2
    ids = jnp.stack([m, c, lax.axis_index("fsdp")]).astype(jnp.int32)
    pair = lambda v: swap(v, "bal", 1)
    near = lambda v: swap(v, "bal", 2)
    far = lambda v: swap(v, "bal", 4)
    cross = lambda v: swap(v, "bal", 6)

    x1, x2 = near(tokens), far(tokens)
    block = (column_of(m, c) // HEAD_DIM).astype(jnp.int32).reshape(1)
    w0, x0 = prepare(ids, block, kv_weight, tokens)
    w2, w1 = swap(w0, "fsdp", 2), swap(w0, "fsdp", 1)
    x1, x2, w1, w2 = lax.optimization_barrier((x1, x2, w1, w2))
    w3 = swap(w2, "fsdp", 1)
    ws = (w0, w1, w2, w3)
    half = on_chip((rows // 2, width))
    p0, *away = cut_heads(ids, queries, out_grad)
    x1, x2, *away = lax.optimization_barrier((x1, x2, *away))
    p1, p2, p3 = away
    top, low = run(cut_kernel, (half, half), (), (x1, x2))
    x3 = [far(top), near(low)]
    flip = lambda vs: [pair(v) for v in vs]
    early = (x0, pair(x0), x1, pair(x1), x2, pair(x2))
    p1, p2 = near(p1), far(p2)
    first = run(project_kernel, on_chip((6 * rows, HEAD_DIM)), (ids,), early + ws)
    *x3, first = lax.optimization_barrier((*x3, first))
    us = tuple(flip(ws))
    late = (*x3, *flip(x3))
    xs = early + late
    p1, p2, p3, first = lax.optimization_barrier((p1, p2, p3, first))
    mine = run(order_kernel, on_chip((8 * rows, HEAD_DIM)), (ids,), late + ws + (first,))
    p3 = cross(p3)
    got = pair(mine)
    (o0,), state = attend((0,), ids, doc_lengths, (mine, got), (p0,))
    p1, p2, *state = lax.optimization_barrier((p1, p2, *state))
    (o1, o2), state = attend((1, 2), ids, doc_lengths, state, (p1, p2))
    o1, o2 = near(o1), far(o2)
    p3, *state = lax.optimization_barrier((p3, *state))
    (o3,), (g_mine, g_keep, g_send) = attend((3,), ids, doc_lengths, state, (p3,), True)
    g_send, us = lax.optimization_barrier((g_send, us))
    g_got = pair(g_send)
    o3 = cross(o3)

    third = on_chip((size, HEAD_DIM))
    half = (rows, width // 2)
    send_a, send_b, keep_a, keep_b = run(
        token_kernel,
        (on_chip((2, *half)), on_chip((2, *half)), on_chip((2, *half), F32), on_chip((2, *half), F32)),
        (ids,),
        (g_mine, g_keep, g_got) + ws + us,
    )
    got_a, got_b = near(send_a), far(send_b)
    keep, *sends = run(
        weight_kernel,
        (on_chip((size, HEAD_DIM), F32), third, third, third),
        (ids,),
        (g_mine, g_got) + xs,
        scratch=[pltpu.VMEM((HEAD_DIM, 8 * rows), BF16)],
    )
    gots = [swap(v, "fsdp", bit) for v, bit in zip(sends, (1, 2, 3))]
    keep = run(add_kernel, on_chip((size, HEAD_DIM), F32), (), (keep, gots[0]))
    mine = run(last_kernel, on_chip((size, HEAD_DIM)), (), (keep, *gots[1:]))
    got_a, got_b, mine = lax.optimization_barrier((got_a, got_b, mine))
    fold = (on_chip(half, F32), on_chip(half))
    a, a_send, b, b_send = run(fold_both_kernel, fold + fold, (), (keep_a, got_a, keep_b, got_b))
    got_a, got_b = far(a_send), near(b_send)
    like = jax.ShapeDtypeStruct(queries.shape, BF16)
    mine = [mine, near(mine), far(mine), cross(mine)]
    mine[1], o1, o2, o3 = lax.optimization_barrier((mine[1], o1, o2, o3))
    attn_out, grad_queries = run(place_kernel, (like, like), (ids,), (o0, o1, o2, o3))
    mine[2], mine[3], attn_out, grad_queries = lax.optimization_barrier((mine[2], mine[3], attn_out, grad_queries))
    theirs = [pair(v) for v in mine]
    grad_weight, grad_tokens = run(
        final_kernel,
        (
            jax.ShapeDtypeStruct((size, kv_weight.shape[1]), F32),
            jax.ShapeDtypeStruct(tokens.shape, BF16),
        ),
        (ids,),
        (*mine, *theirs, a, got_a, b, got_b),
    )
    return attn_out, grad_queries, grad_tokens, grad_weight


def from_behind(value, axis, steps):
    count = lax.axis_size(axis)
    initial, last = (max(0, -steps), min(count, count - steps))
    return lax.ppermute(value, axis, [(source, source + steps) for source in range(initial, last)])


def doc_index(doc_ends, positions):
    return jnp.sum((doc_ends[None, :] <= positions[:, None]).astype(jnp.int32), axis=1)


def score_tile(q_group, key_block, mask_block, inv_root):
    raw_scores = (
        jnp.einsum("qhd,kd->hqk", q_group, key_block, preferred_element_type=jnp.float32) * inv_root
    )
    return jnp.where(mask_block[None], raw_scores, NEG_FILL)


def value_tile(prob_tile, value_block):
    return jnp.einsum("hqk,kd->qhd", prob_tile, value_block, preferred_element_type=jnp.float32)


def dprob_tile(grad_group, value_block):
    return jnp.einsum("qhd,kd->hqk", grad_group, value_block, preferred_element_type=jnp.float32)


def query_tile(dscore_tile, key_block):
    return jnp.einsum("hqk,kd->qhd", dscore_tile, key_block, preferred_element_type=jnp.float32)


def key_tile(dscore_tile, q_group, inv_root):
    return (
        jnp.einsum("hqk,qhd->kd", dscore_tile, q_group, preferred_element_type=jnp.float32)
        * inv_root
    )


def value_grad_tile(prob_tile, grad_group):
    return jnp.einsum("hqk,qhd->kd", prob_tile, grad_group, preferred_element_type=jnp.float32)


def attend_rows(q_rows, kv_blocks, grad_rows, allowed_parts):
    row_count = q_rows.shape[0]
    key_rows = kv_blocks[0].shape[0]
    group_size = HEADS // KV_HEADS
    inv_root = HEAD_DIM ** (-0.5)
    window_range = list(range(len(kv_blocks)))
    row_shape = (row_count, group_size, HEAD_DIM)
    out_parts = []
    dq_parts = []
    key_grads = [[] for window_pos in window_range]
    value_grads = [[] for window_pos in window_range]
    for head_group in range(KV_HEADS):
        col_start = head_group * group_size * HEAD_DIM
        col_stop = col_start + group_size * HEAD_DIM
        val_start = (KV_HEADS + head_group) * HEAD_DIM
        q_group = q_rows[:, col_start:col_stop].reshape(row_shape)
        grad_group = grad_rows[:, col_start:col_stop].reshape(row_shape)
        key_list = [
            piece[:, head_group * HEAD_DIM : (head_group + 1) * HEAD_DIM] for piece in kv_blocks
        ]
        value_list = [piece[:, val_start : val_start + HEAD_DIM] for piece in kv_blocks]
        score_tiles = [
            score_tile(q_group, key_list[window_pos], allowed_parts[window_pos], inv_root)
            for window_pos in window_range
        ]
        scores = jnp.concatenate(score_tiles, axis=2)
        row_max = jnp.max(scores, axis=-1, keepdims=True)
        exp_shift = jnp.exp(scores - row_max)
        prob_full = exp_shift / jnp.sum(exp_shift, axis=-1, keepdims=True)
        prob_low = prob_full.astype(jnp.bfloat16)
        prob_tiles = [
            prob_low[:, :, window_pos * key_rows : (window_pos + 1) * key_rows]
            for window_pos in window_range
        ]
        out_accum = jnp.zeros(row_shape, jnp.float32)
        for window_pos in window_range:
            out_accum = out_accum + value_tile(prob_tiles[window_pos], value_list[window_pos])
        out_group = out_accum.astype(jnp.bfloat16)
        row_delta = jnp.sum(grad_group.astype(jnp.float32) * out_group.astype(jnp.float32), axis=-1)
        dprob_tiles = [
            dprob_tile(grad_group, value_list[window_pos]) for window_pos in window_range
        ]
        dprobs = jnp.concatenate(dprob_tiles, axis=2)
        dscores = (prob_full * (dprobs - row_delta.T[:, :, None])).astype(jnp.bfloat16)
        dq_accum = jnp.zeros(row_shape, jnp.float32)
        for window_pos in window_range:
            dscore_piece = dscores[:, :, window_pos * key_rows : (window_pos + 1) * key_rows]
            dq_accum = dq_accum + query_tile(dscore_piece, key_list[window_pos])
            key_grads[window_pos].append(key_tile(dscore_piece, q_group, inv_root))
            value_grads[window_pos].append(value_grad_tile(prob_tiles[window_pos], grad_group))
        dq_group = (dq_accum * inv_root).astype(jnp.bfloat16)
        out_parts.append(out_group.reshape(row_count, group_size * HEAD_DIM))
        dq_parts.append(dq_group.reshape(row_count, group_size * HEAD_DIM))
    window_terms = [
        jnp.concatenate(key_grads[window_pos] + value_grads[window_pos], axis=1)
        for window_pos in window_range
    ]
    return (jnp.concatenate(out_parts, axis=1), jnp.concatenate(dq_parts, axis=1), window_terms)


def local(tokens, kv_weight, queries, out_grad, doc_lengths):
    row_count = tokens.shape[0]
    bal_index = lax.axis_index("bal")
    doc_ends = jnp.cumsum(doc_lengths[0])
    row_ids = jnp.arange(row_count, dtype=jnp.int32)
    own_pos = bal_index * row_count + row_ids
    own_doc = doc_index(doc_ends, own_pos)
    allowed_parts = []
    for distance in range(REACH, -1, -1):
        key_pos = (bal_index - distance) * row_count + row_ids
        key_doc = jnp.where(key_pos >= 0, doc_index(doc_ends, key_pos), -1)
        allowed_parts.append(
            (own_doc[:, None] == key_doc[None, :]) & (key_pos[None, :] <= own_pos[:, None])
        )
    full_weight = lax.all_gather(kv_weight, "fsdp", axis=0, tiled=True)
    kv_accum = jnp.dot(tokens, full_weight, preferred_element_type=jnp.float32)
    kv_rows = kv_accum.astype(jnp.bfloat16)
    earlier = [kv_rows]
    for distance in range(1, REACH + 1):
        earlier.append(from_behind(kv_rows, "bal", distance))
    kv_blocks = earlier[::-1]
    attn_out, grad_queries, window_terms = attend_rows(queries, kv_blocks, out_grad, allowed_parts)
    grad_terms = window_terms[::-1]
    grad_sum = grad_terms[0]
    for distance in range(1, REACH + 1):
        grad_sum = grad_sum + from_behind(
            grad_terms[distance].astype(jnp.bfloat16), "bal", -distance
        ).astype(jnp.float32)
    grad_kv = grad_sum.astype(jnp.bfloat16)
    grad_tokens = lax.dot_general(
        grad_kv, full_weight, (((1,), (1,)), ((), ())), preferred_element_type=jnp.float32
    ).astype(jnp.bfloat16)
    shard_sum = lax.psum_scatter(
        lax.dot_general(
            tokens, grad_kv, (((0,), (0,)), ((), ())), preferred_element_type=jnp.float32
        ).astype(jnp.bfloat16),
        "fsdp",
        scatter_dimension=0,
        tiled=True,
    )
    grad_weight = lax.psum(shard_sum, "bal").astype(jnp.float32)
    return (attn_out, grad_queries, grad_tokens, grad_weight)


def solution(mesh):
    placed = (
        P(("fsdp", "bal"), None),
        P("fsdp", None),
        P(("fsdp", "bal"), None),
        P(("fsdp", "bal"), None),
        P("fsdp", None),
    )
    one_plane = mesh.shape["bal"] == 8 and mesh.shape["fsdp"] == 4
    return jax.shard_map(
        plane_local if one_plane else local,
        mesh=mesh,
        in_specs=placed,
        out_specs=(
            P(("fsdp", "bal"), None),
            P(("fsdp", "bal"), None),
            P(("fsdp", "bal"), None),
            P("fsdp", None),
        ),
        check_vma=False,
    )
```
